32 devices in a mesh: dp: 8 (over z, x), tensor: 4 (over y, core).
Axes of the slice: x: 2, y: 2, z: 4, core: 2. Of those that a mesh axis runs over, the one named last changes fastest.
Arguments:
- cells_x: bfloat16 [16384, 768], P(('dp', 'tensor')), may hold values from -6 to 6
- cotangent: bfloat16 [16384, 768], P(('dp', 'tensor')), may hold values from -6 to 6
- gene_counts: int32 [8], replicated, may hold values from 300 to 2048, as said below
- slot_cell: int32 [8], P('dp'), may hold values from 0 to 7, each once
- norm_gain: bfloat16 [2, 768], replicated, may hold values from 0.5 to 1.5
- norm_shift: bfloat16 [2, 768], replicated, may hold values from -1 to 1
- out_bias: bfloat16 [2, 768], replicated, may hold values from -1 to 1
- w_qkv: bfloat16 [3, 768, 768], P(None, None, 'tensor'), may hold values from -0.3125 to 0.3125
- qv_bias: bfloat16 [2, 768], P(None, 'tensor'), may hold values from -1.5 to 1.5
- w_out: bfloat16 [768, 768], P('tensor'), may hold values from -1.75 to 1.75
- w_up: bfloat16 [768, 3072], P(None, 'tensor'), may hold values from -0.21875 to 0.21875
- up_bias: bfloat16 [3072], P('tensor'), may hold values from -1.5 to 1.5
- w_down: bfloat16 [3072, 768], P('tensor'), may hold values from -0.109375 to 0.109375
Outputs:
- block_out: bfloat16 [16384, 768], P(('dp', 'tensor'))
- input_grad: bfloat16 [16384, 768], P(('dp', 'tensor'))
- grad_norm_gain: float32 [2, 768], replicated
- grad_norm_shift: float32 [2, 768], replicated
- grad_out_bias: float32 [2, 768], replicated
- grad_qkv: float32 [3, 768, 768], P(None, None, 'tensor')
- grad_qv_bias: float32 [2, 768], P(None, 'tensor')
- grad_w_out: float32 [768, 768], P('tensor')
- grad_w_up: float32 [768, 3072], P(None, 'tensor')
- grad_up_bias: float32 [3072], P('tensor')
- grad_w_down: float32 [3072, 768], P('tensor')
The draws below stay inside these ranges and needn't reach their ends.
Inputs may be any that keep to these rules, and one draw needn't show every extreme that they name: `gene_counts`: some cell has exactly 2048 expressed genes and some exactly 300. `slot_cell`: every cell is held in exactly one slot.
All inputs are finite; a program needn't handle non-finite values.
Results may differ from the reference program's by a relative error of at most 0.013.
The reference program's roundings to bfloat16 on the way count: a program that leaves them out, or rounds other values in their place, can miss the bound.
Values may be sent and summed in bfloat16 or wider, within the bound.
No kernel may reach another device: no remote copies, remote signals or barrier semaphores. Data moves between devices by JAX's collectives and lax.ppermute only.
A program may use at most 128 MiB of HBM per device.

```python
import jax
import jax.numpy as jnp
from jax import lax

D = 768
HEADS = 12
HEAD_DIM = 64
FF = 3072
SLOT = 2048
MIN_GENES = 300
CELLS = 8
TOKENS = 16384


def draw_gene_counts(key, part):
    key_counts = jax.random.fold_in(key, 11)
    key_spots = jax.random.fold_in(key, 12)
    counts = jax.random.randint(key_counts, (CELLS,), MIN_GENES, SLOT + 1)
    chosen = jax.random.permutation(key_spots, CELLS)
    counts = counts.at[chosen[0]].set(SLOT)
    counts = counts.at[chosen[1]].set(MIN_GENES)
    return counts.astype(jnp.int32)


def block_scale(stream_key, shape, cuts, low, top_value):
    loudness = 1.0
    for dim, blocks in cuts:
        draws = jax.random.uniform(jax.random.fold_in(jax.random.fold_in(stream_key, 6), dim), (blocks,), jnp.float32, low / len(cuts), top_value / len(cuts))
        loudness = loudness * jnp.repeat(jnp.exp(draws), shape[dim] // blocks).reshape((-1,) + (1,) * (len(shape) - 1 - dim))
    return loudness


def noise(stream_key, shape, width, bound, pieces=(), kind=jnp.bfloat16):
    array = jax.random.normal(stream_key, shape, jnp.float32) * width
    if len(pieces) > 0:
        array = block_scale(stream_key, shape, pieces, -0.22, 0.18) * array
    return jnp.clip(array, min=-bound, max=bound).astype(kind)


def setup_inputs(seed: int = 0) -> dict:
    splits = jax.random.split(jax.random.key(seed), 14)
    cells_x = noise(splits[0], (TOKENS, D), 1.0, 6.0, ((0, 32),))
    cotangent = noise(splits[1], (TOKENS, D), 1.0, 6.0, ((0, 32),))
    gene_counts = draw_gene_counts(jax.random.fold_in(splits[13], 71), 0)
    slot_cell = jax.random.permutation(splits[3], CELLS).astype(jnp.int32)
    norm_gain = jnp.clip(1.0 + 0.1 * jax.random.normal(splits[4], (2, D), jnp.float32), 0.5, 1.5).astype(jnp.bfloat16)
    norm_shift = noise(splits[5], (2, D), 0.2, 1.0)
    out_bias = noise(splits[6], (2, D), 0.2, 1.0)
    w_qkv = noise(splits[7], (3, D, D), (D // 2) ** -0.5, 0.3125, ((2, 4),))
    qv_bias = noise(splits[8], (2, D), 0.3, 1.5, ((1, 4),))
    w_out = noise(splits[9], (D, D), (D // 64) ** -0.5, 1.75, ((0, 4),))
    w_up = noise(splits[10], (D, FF), D ** -0.5, 0.21875, ((1, 4),))
    up_bias = noise(splits[11], (FF,), 0.3, 1.5, ((0, 4),))
    w_down = noise(splits[12], (FF, D), FF ** -0.5, 0.109375, ((0, 4),))
    return dict(cells_x=cells_x, cotangent=cotangent, gene_counts=gene_counts, slot_cell=slot_cell, norm_gain=norm_gain, norm_shift=norm_shift, out_bias=out_bias, w_qkv=w_qkv, qv_bias=qv_bias, w_out=w_out, w_up=w_up, up_bias=up_bias, w_down=w_down)


EPSILON = 1e-05
NEGATIVE = -1e+30

@jax.custom_vjp
def low(v):
    return lax.optimization_barrier(v.astype(jnp.bfloat16)).astype(jnp.float32)

@jax.custom_vjp
def low_back(v):
    return v

def low_keep(v):
    return (low(v), None)

def low_pass(kept, grad):
    return (grad,)

def back_keep(v):
    return (v, None)

def back_low(kept, grad):
    return (low(grad),)
low.defvjp(low_keep, low_pass)
low_back.defvjp(back_keep, back_low)

def exact_gelu(hidden):
    return jax.nn.gelu(hidden, approximate=False)

def normalize(features, gain_row, shift_row):
    row_mean = lax.optimization_barrier(jnp.mean(features, axis=-1, keepdims=True))
    centered = features - row_mean
    variance = lax.optimization_barrier(jnp.mean(centered * centered, axis=-1, keepdims=True))
    return centered * lax.rsqrt(variance + EPSILON) * gain_row + shift_row

def product(left, right):
    return jnp.dot(left, right, preferred_element_type=jnp.float32, precision=lax.Precision.HIGHEST)

def cell_attention(query_heads, key_heads, value_heads, live_keys):
    raw_scores = jnp.einsum('qhe,khe->hqk', query_heads, key_heads, precision=lax.Precision.HIGHEST)
    scores = low_back(raw_scores) * HEAD_DIM ** (-0.5)
    scores = jnp.where(live_keys[None, None, :], scores, NEGATIVE)
    softmaxed = low(jax.nn.softmax(scores, axis=-1))
    attended = jnp.einsum('hqk,khe->qhe', softmaxed, value_heads, precision=lax.Precision.HIGHEST)
    return attended.reshape(query_heads.shape[0], -1)

def forward(inputs, norm_gain, norm_shift, out_bias, w_qkv, qv_bias, w_out, w_up, up_bias, w_down, live_rows, live_keys):
    normed_in = low(normalize(inputs, norm_gain[0], norm_shift[0]))
    projected = jnp.einsum('rd,sdc->src', normed_in, w_qkv, precision=lax.Precision.HIGHEST)
    bias_rows = jnp.stack([qv_bias[0], jnp.zeros_like(qv_bias[0]), qv_bias[1]])
    projected = low(low_back(projected + bias_rows[:, None, :]))
    head_parts = projected.reshape(3, CELLS, SLOT, HEADS, HEAD_DIM)
    checked = jax.checkpoint(cell_attention)
    attended = lax.map(lambda packed: checked(packed[0], packed[1], packed[2], packed[3]), (head_parts[0], head_parts[1], head_parts[2], live_keys))
    attended = low(low_back(attended.reshape(TOKENS, D)))
    middle = inputs + low_back(product(attended, w_out)) + out_bias[0]
    normed_mid = low(normalize(middle, norm_gain[1], norm_shift[1]))
    hidden = low_back(product(normed_mid, w_up) + up_bias)
    active = low(exact_gelu(hidden))
    output = middle + product(active, w_down) + out_bias[1]
    return jnp.where(live_rows[:, None], output, 0.0)

def reference(cells_x, cotangent, gene_counts, slot_cell, norm_gain, norm_shift, out_bias, w_qkv, qv_bias, w_out, w_up, up_bias, w_down):
    lengths = gene_counts[slot_cell]
    positions = jnp.arange(SLOT, dtype=jnp.int32)
    live_keys = positions[None, :] < lengths[:, None]
    live_rows = live_keys.reshape(TOKENS)
    floats = [operand.astype(jnp.float32) for operand in (cells_x, norm_gain, norm_shift, out_bias, w_qkv, qv_bias, w_out, w_up, up_bias, w_down)]

    def layer_fn(*params):
        return forward(*params, live_rows, live_keys)
    output, pullback = jax.vjp(layer_fn, *floats)
    gradients = pullback(cotangent.astype(jnp.float32))
    return (output.astype(jnp.bfloat16), gradients[0].astype(jnp.bfloat16), gradients[1], gradients[2], gradients[3], gradients[4], gradients[5], gradients[6], gradients[7], gradients[8], gradients[9])
```

```python
import jax
import jax.numpy as jnp
from jax import lax
from jax.sharding import PartitionSpec as P

HEAD_DIM = 64
SLOT = 2048


EPSILON = 1e-05
NEGATIVE = -1e30


def exact_gelu(hidden):
    return jax.nn.gelu(hidden, approximate=False)


def normalize(features, gain_row, shift_row):
    row_mean = jnp.mean(features, axis=-1, keepdims=True)
    centered = features - row_mean
    variance = jnp.mean(centered * centered, axis=-1, keepdims=True)
    inverse = lax.rsqrt(variance + EPSILON)
    scaled = centered * inverse
    return (scaled * gain_row.astype(jnp.float32) + shift_row.astype(jnp.float32), scaled, inverse)


def normalize_back(upstream, scaled, inverse, gain_row):
    graded = upstream * gain_row.astype(jnp.float32)
    grad_mean = jnp.mean(graded, axis=-1, keepdims=True)
    cross_mean = jnp.mean(graded * scaled, axis=-1, keepdims=True)
    return (
        inverse * (graded - grad_mean - scaled * cross_mean),
        jnp.sum(upstream * scaled, axis=0),
        jnp.sum(upstream, axis=0),
    )


def contract_last(left, right):
    return lax.dot_general(
        left, right, (((1,), (1,)), ((), ())), preferred_element_type=jnp.float32
    )


def contract_first(left, right):
    return lax.dot_general(
        left, right, (((0,), (0,)), ((), ())), preferred_element_type=jnp.float32
    )


def masked_scores(block_queries, key_heads, live_keys, score_scale):
    scores = (
        jnp.einsum("qhe,khe->hqk", block_queries, key_heads, preferred_element_type=jnp.float32)
        * score_scale
    )
    return jnp.where(live_keys[None, None, :], scores, NEGATIVE)


def attend_cell(query_heads, key_heads, value_heads, live_keys, block_rows):
    score_scale = query_heads.shape[-1] ** (-0.5)

    def one_block(block_index):
        block_queries = lax.dynamic_slice_in_dim(
            query_heads, block_index * block_rows, block_rows, 0
        )
        scores = masked_scores(block_queries, key_heads, live_keys, score_scale)
        row_max = jnp.max(scores, axis=-1, keepdims=True)
        exp_scores = jnp.exp(scores - row_max)
        row_total = jnp.sum(exp_scores, axis=-1, keepdims=True)
        soft_low = (exp_scores / row_total).astype(jnp.bfloat16)
        attended = jnp.einsum(
            "hqk,khe->qhe", soft_low, value_heads, preferred_element_type=jnp.float32
        )
        return (attended, (row_max + jnp.log(row_total))[..., 0])

    attended, log_totals = lax.map(one_block, jnp.arange(query_heads.shape[0] // block_rows))
    return (attended.reshape(query_heads.shape[0], -1), log_totals)


def attend_back(query_heads, key_heads, value_heads, grad_heads, log_totals, live_keys, block_rows):
    score_scale = query_heads.shape[-1] ** (-0.5)
    slot_rows = query_heads.shape[0]

    def one_block(sums_carry, block_index):
        key_sum, value_sum = sums_carry
        first_row = block_index * block_rows
        block_queries = lax.dynamic_slice_in_dim(query_heads, first_row, block_rows, 0)
        block_grads = lax.dynamic_slice_in_dim(grad_heads, first_row, block_rows, 0)
        scores = masked_scores(block_queries, key_heads, live_keys, score_scale)
        softmaxed = jnp.exp(scores - log_totals[block_index][..., None])
        soft_low = softmaxed.astype(jnp.bfloat16)
        prob_grad = jnp.einsum(
            "qhe,khe->hqk", block_grads, value_heads, preferred_element_type=jnp.float32
        )
        row_inner = jnp.sum(softmaxed * prob_grad, axis=-1, keepdims=True)
        score_grad = (score_scale * softmaxed * (prob_grad - row_inner)).astype(jnp.bfloat16)
        query_grad = jnp.einsum(
            "hqk,khe->qhe", score_grad, key_heads, preferred_element_type=jnp.float32
        )
        key_sum = key_sum + jnp.einsum(
            "hqk,qhe->khe", score_grad, block_queries, preferred_element_type=jnp.float32
        )
        value_sum = value_sum + jnp.einsum(
            "hqk,qhe->khe", soft_low, block_grads, preferred_element_type=jnp.float32
        )
        return ((key_sum, value_sum), query_grad)

    zero_heads = jnp.zeros(key_heads.shape, jnp.float32)
    (key_sum, value_sum), query_grad = lax.scan(
        one_block, (zero_heads, zero_heads), jnp.arange(slot_rows // block_rows)
    )
    return (
        query_grad.reshape(slot_rows, -1).astype(jnp.bfloat16),
        key_sum.reshape(slot_rows, -1).astype(jnp.bfloat16),
        value_sum.reshape(slot_rows, -1).astype(jnp.bfloat16),
    )


def pair_swap(array, axis, bit):
    size = lax.axis_size(axis)
    return lax.ppermute(array, axis, [(source, source ^ bit) for source in range(size)])


def gather_relative(rows):
    across = pair_swap(rows, "tensor", 2)
    beside = pair_swap(rows, "tensor", 1)
    return (rows, beside, across, pair_swap(across, "tensor", 1))


def scatter_relative(blocks):
    low = [block.astype(jnp.bfloat16) for block in blocks]
    far = blocks[2] + pair_swap(low[3], "tensor", 1).astype(jnp.float32)
    far_low = pair_swap(far.astype(jnp.bfloat16), "tensor", 2)
    near = blocks[0] + pair_swap(low[1], "tensor", 1).astype(jnp.float32)
    return near + far_low.astype(jnp.float32)


def reduce_cells(grads, bits):
    index = lax.axis_index("dp")
    block = grads
    for bit in bits:
        half = block.shape[0] // 2
        side = (index // bit) % 2
        kept = lax.dynamic_slice_in_dim(block, side * half, half, 0)
        sent = lax.dynamic_slice_in_dim(block, (1 - side) * half, half, 0)
        got = pair_swap(sent.astype(jnp.bfloat16), "dp", bit)
        block = kept + got.astype(jnp.float32)
    block = block.astype(jnp.bfloat16)
    for bit in reversed(bits):
        side = (index // bit) % 2
        got = pair_swap(block, "dp", bit)
        block = jnp.where(
            side == 0, jnp.concatenate([block, got]), jnp.concatenate([got, block])
        )
    return block.astype(jnp.float32)


def sum_cells(grads):
    bits = [1 << step for step in range((lax.axis_size("dp") - 1).bit_length())]
    half = grads.shape[0] // 2
    rotated = bits[1:] + bits[:1]
    return jnp.concatenate([reduce_cells(grads[:half], bits), reduce_cells(grads[half:], rotated)])


def sum_small(rows, axes):
    for axis in axes:
        bit = 1
        while bit < lax.axis_size(axis):
            rows = rows + pair_swap(rows, axis, bit)
            bit *= 2
    return rows


def per_device(
    cells_x,
    cotangent,
    gene_counts,
    slot_cell,
    norm_gain,
    norm_shift,
    out_bias,
    w_qkv,
    qv_bias,
    w_out,
    w_up,
    up_bias,
    w_down,
):
    rows = cells_x.shape[0]
    width = cells_x.shape[1]
    place = lax.axis_index("tensor")
    cell_ids = jnp.arange(gene_counts.shape[0], dtype=jnp.int32)
    length = jnp.sum(jnp.where(slot_cell[0] == cell_ids, gene_counts, 0))
    positions = jnp.concatenate(
        [(place ^ block) * rows + jnp.arange(rows, dtype=jnp.int32) for block in range(4)]
    )
    live_keys = positions < length
    live_rows = live_keys[:rows]
    x_rows = jnp.concatenate(gather_relative(cells_x))
    out_grad = jnp.where(live_rows[:, None], cotangent, jnp.zeros_like(cotangent))
    grad_rows = jnp.concatenate(gather_relative(out_grad))
    normed_in, scaled_in, inverse_in = normalize(
        x_rows.astype(jnp.float32), norm_gain[0], norm_shift[0]
    )
    gathered_in = normed_in.astype(jnp.bfloat16)
    bias_rows = jnp.stack([qv_bias[0], jnp.zeros_like(qv_bias[0]), qv_bias[1]]).astype(jnp.float32)
    projected = jnp.einsum("rd,sdc->src", gathered_in, w_qkv, preferred_element_type=jnp.float32)
    projected = (projected + bias_rows[:, None, :]).astype(jnp.bfloat16)
    heads_local = projected.shape[2] // HEAD_DIM
    head_parts = projected.reshape(3, SLOT, heads_local, HEAD_DIM)
    attended, log_totals = attend_cell(head_parts[0], head_parts[1], head_parts[2], live_keys, rows)
    attended_low = attended.astype(jnp.bfloat16)

    def cut(array):
        return [array[block * rows : (block + 1) * rows] for block in range(4)]

    attn_sum = scatter_relative(
        cut(jnp.dot(attended_low, w_out, preferred_element_type=jnp.float32))
    )
    middle = cells_x.astype(jnp.float32) + attn_sum + out_bias[0].astype(jnp.float32)
    normed_mid, scaled_mid, inverse_mid = normalize(middle, norm_gain[1], norm_shift[1])
    ffn_rows = jnp.concatenate(gather_relative(normed_mid.astype(jnp.bfloat16)))
    hidden = jnp.dot(ffn_rows, w_up, preferred_element_type=jnp.float32) + up_bias.astype(
        jnp.float32
    )
    active, gelu_back = jax.vjp(exact_gelu, hidden)
    active_low = active.astype(jnp.bfloat16)
    hidden_grad = gelu_back(contract_last(grad_rows, w_down))[0].astype(jnp.bfloat16)
    mid_norm_grad = scatter_relative(cut(contract_last(hidden_grad, w_up)))
    branch = scatter_relative(cut(jnp.dot(active_low, w_down, preferred_element_type=jnp.float32)))
    output = jnp.where(live_rows[:, None], middle + branch + out_bias[1].astype(jnp.float32), 0.0)
    block_out = output.astype(jnp.bfloat16)
    down_grad = contract_first(active_low, grad_rows)
    up_grad = contract_first(ffn_rows, hidden_grad)
    up_bias_grad = jnp.sum(hidden_grad, axis=0, dtype=jnp.float32)
    mid_back, gain_mid, shift_mid = normalize_back(
        mid_norm_grad, scaled_mid, inverse_mid, norm_gain[1]
    )
    middle_grad = out_grad.astype(jnp.float32) + mid_back
    middle_rows = jnp.concatenate(gather_relative(middle_grad.astype(jnp.bfloat16)))
    ffn_grads = sum_cells(jnp.concatenate([up_grad, down_grad]))
    up_grad, down_grad = ffn_grads[: up_grad.shape[0]], ffn_grads[up_grad.shape[0] :]
    attended_grad = contract_last(middle_rows, w_out).astype(jnp.bfloat16)
    out_weight_grad = contract_first(attended_low, middle_rows)
    grad_heads = attended_grad.reshape(SLOT, heads_local, HEAD_DIM)
    query_grad, key_grad, value_grad = attend_back(
        head_parts[0], head_parts[1], head_parts[2], grad_heads, log_totals, live_keys, rows
    )
    qkv_grad = jnp.stack([query_grad, key_grad, value_grad])
    in_norm_part = jnp.einsum("src,sdc->rd", qkv_grad, w_qkv, preferred_element_type=jnp.float32)
    in_norm_grad = scatter_relative(cut(in_norm_part))
    qkv_weight_grad = jnp.einsum(
        "rd,src->sdc", gathered_in, qkv_grad, preferred_element_type=jnp.float32
    )
    query_bias = jnp.sum(qkv_grad[0], axis=0, dtype=jnp.float32)
    value_bias = jnp.sum(qkv_grad[2], axis=0, dtype=jnp.float32)
    own = slice(0, rows)
    in_back, _, _ = normalize_back(in_norm_grad, scaled_in[own], inverse_in[own], norm_gain[0])
    input_grad = (middle_grad + in_back).astype(jnp.bfloat16)
    shared = sum_small(
        jnp.stack(
            [
                jnp.sum(in_norm_part * scaled_in, axis=0),
                gain_mid,
                jnp.sum(in_norm_part, axis=0),
                shift_mid,
                jnp.sum(middle_grad, axis=0),
                jnp.sum(out_grad, axis=0, dtype=jnp.float32),
            ]
        ),
        ("tensor", "dp"),
    )
    sharded = sum_small(jnp.concatenate([up_bias_grad, query_bias, value_bias])[None], ("dp",))[0]
    columns = w_qkv.shape[2]
    attn_grads = sum_cells(
        jnp.concatenate([out_weight_grad, qkv_weight_grad.reshape(-1, width)])
    )
    out_weight_grad = attn_grads[:columns]
    qkv_weight_grad = attn_grads[columns:].reshape(w_qkv.shape)
    units = up_bias.shape[0]
    return (
        block_out,
        input_grad,
        shared[0:2],
        shared[2:4],
        shared[4:6],
        qkv_weight_grad,
        sharded[units:].reshape(2, columns),
        out_weight_grad,
        up_grad,
        sharded[:units],
        down_grad,
    )


def solution(mesh):
    return jax.shard_map(
        per_device,
        mesh=mesh,
        in_specs=(
            P(("dp", "tensor"), None),
            P(("dp", "tensor"), None),
            P(),
            P("dp"),
            P(),
            P(),
            P(),
            P(None, None, "tensor"),
            P(None, "tensor"),
            P("tensor", None),
            P(None, "tensor"),
            P("tensor"),
            P("tensor", None),
        ),
        out_specs=(
            P(("dp", "tensor"), None),
            P(("dp", "tensor"), None),
            P(),
            P(),
            P(),
            P(None, None, "tensor"),
            P(None, "tensor"),
            P("tensor", None),
            P(None, "tensor"),
            P("tensor"),
            P("tensor", None),
        ),
        check_vma=False,
    )
```

```python
import jax
import jax.numpy as jnp
from jax import lax
from jax.experimental import pallas as pl
from jax.experimental.pallas import tpu as pltpu
from jax.sharding import PartitionSpec as P

HEAD_DIM = 64
SLOT = 2048


EPSILON = 1e-05
NEGATIVE = -1e30
FORWARD_STEPS = 4
BACKWARD_STEPS = 4


def exact_gelu(hidden):
    return jax.nn.gelu(hidden, approximate=False)


def normalize(features, gain_row, shift_row):
    row_mean = jnp.mean(features, axis=-1, keepdims=True)
    centered = features - row_mean
    variance = jnp.mean(centered * centered, axis=-1, keepdims=True)
    inverse = lax.rsqrt(variance + EPSILON)
    scaled = centered * inverse
    return (scaled * gain_row.astype(jnp.float32) + shift_row.astype(jnp.float32), scaled, inverse)


def normalize_back(upstream, scaled, inverse, gain_row):
    graded = upstream * gain_row.astype(jnp.float32)
    grad_mean = jnp.mean(graded, axis=-1, keepdims=True)
    cross_mean = jnp.mean(graded * scaled, axis=-1, keepdims=True)
    return (
        inverse * (graded - grad_mean - scaled * cross_mean),
        jnp.sum(upstream * scaled, axis=0),
        jnp.sum(upstream, axis=0),
    )


def contract_last(left, right):
    return lax.dot_general(
        left, right, (((1,), (1,)), ((), ())), preferred_element_type=jnp.float32
    )


def contract_first(left, right):
    return lax.dot_general(
        left, right, (((0,), (0,)), ((), ())), preferred_element_type=jnp.float32
    )


def transpose_low(array):
    return jnp.transpose(array.astype(jnp.float32)).astype(jnp.bfloat16)


def fill_heads(scalars, projected, keys_aug, queries_aug):
    heads, slot_rows, _ = keys_aug.shape
    rows = slot_rows // 4
    scale = HEAD_DIM ** (-0.5)
    column = lax.broadcasted_iota(jnp.int32, (rows, HEAD_DIM), 1)
    row = lax.broadcasted_iota(jnp.int32, (rows, HEAD_DIM), 0)
    ones = jnp.where(column == 0, 1.0, 0.0).astype(jnp.bfloat16)
    for block in range(4):
        part = pl.ds(block * rows, rows)
        dead = (scalars[1 + block] + row) >= scalars[0]
        bias = jnp.where(jnp.logical_and(dead, column == 0), NEGATIVE, 0.0).astype(jnp.bfloat16)
        queries = (projected[0, part, :].astype(jnp.float32) * scale).astype(jnp.bfloat16)
        keys = projected[1, part, :]
        for head in range(heads):
            cols = slice(head * HEAD_DIM, (head + 1) * HEAD_DIM)
            queries_aug[head, part, :] = jnp.concatenate([queries[:, cols], ones], axis=1)
            keys_aug[head, part, :] = jnp.concatenate([keys[:, cols], bias], axis=1)


def attend_kernel(
    scalars, projected, attended, log_totals, keys_aug, queries_aug, values_t, result
):
    head, step = pl.program_id(0), pl.program_id(1)
    heads, slot_rows, _ = keys_aug.shape
    block = slot_rows // pl.num_programs(1)

    @pl.when(jnp.logical_and(head == 0, step == 0))
    def _():
        fill_heads(scalars, projected, keys_aug, queries_aug)
        extra = lax.broadcasted_iota(jnp.int32, (16, slot_rows), 0)
        ones = jnp.where(extra == 0, 1.0, 0.0).astype(jnp.bfloat16)
        for each in range(heads):
            cols = slice(each * HEAD_DIM, (each + 1) * HEAD_DIM)
            values_t[each, :HEAD_DIM, :] = transpose_low(projected[2, :, cols])
            values_t[each, HEAD_DIM:, :] = ones

    part = pl.ds(pl.multiple_of(step * block, block), block)
    scores = contract_last(keys_aug[head], queries_aug[head, part, :])
    row_max = jnp.max(scores, axis=0, keepdims=True)
    probs = jnp.exp(scores - row_max).astype(jnp.bfloat16)
    mixed = jnp.dot(values_t[head], probs, preferred_element_type=jnp.float32)
    total = mixed[HEAD_DIM : HEAD_DIM + 1, :]
    result[head, part, :] = jnp.transpose(mixed[:HEAD_DIM, :] / total).astype(jnp.bfloat16)
    log_totals[head, :, part] = row_max + jnp.log(total)

    @pl.when(jnp.logical_and(head == heads - 1, step == pl.num_programs(1) - 1))
    def _():
        attended[...] = jnp.concatenate([result[each] for each in range(heads)], axis=1)


def attend_forward(scalars, projected):
    _, slot_rows, columns = projected.shape
    heads = columns // HEAD_DIM
    whole = pl.BlockSpec(memory_space=pltpu.VMEM)
    return pl.pallas_call(
        attend_kernel,
        grid_spec=pltpu.PrefetchScalarGridSpec(
            num_scalar_prefetch=1,
            grid=(heads, FORWARD_STEPS),
            in_specs=[whole],
            out_specs=[whole, whole],
            scratch_shapes=[
                pltpu.VMEM((heads, slot_rows, 128), jnp.bfloat16),
                pltpu.VMEM((heads, slot_rows, 128), jnp.bfloat16),
                pltpu.VMEM((heads, HEAD_DIM + 16, slot_rows), jnp.bfloat16),
                pltpu.VMEM((heads, slot_rows, HEAD_DIM), jnp.bfloat16),
            ],
        ),
        out_shape=[
            jax.ShapeDtypeStruct((slot_rows, columns), jnp.bfloat16),
            jax.ShapeDtypeStruct((heads, 1, slot_rows), jnp.float32),
        ],
        compiler_params=pltpu.CompilerParams(vmem_limit_bytes=60 << 20),
        cost_estimate=pl.CostEstimate(
            flops=4 * heads * slot_rows * slot_rows * 256,
            bytes_accessed=5 * slot_rows * columns * 2,
            transcendentals=heads * slot_rows * slot_rows,
        ),
        name="attend_forward",
    )(scalars, projected)


def attend_back_kernel(
    scalars,
    projected,
    attended,
    attended_grad,
    log_totals,
    grads,
    keys_aug,
    queries_aug,
    keys_t,
    values,
    upstream,
    inner,
    query_sum,
    key_sum,
    value_sum,
):
    head, step = pl.program_id(0), pl.program_id(1)
    heads, slot_rows, _ = keys_aug.shape
    block = slot_rows // pl.num_programs(1)

    @pl.when(jnp.logical_and(head == 0, step == 0))
    def _():
        fill_heads(scalars, projected, keys_aug, queries_aug)
        key_sum[...] = jnp.zeros_like(key_sum)
        value_sum[...] = jnp.zeros_like(value_sum)
        for each in range(heads):
            cols = slice(each * HEAD_DIM, (each + 1) * HEAD_DIM)
            keys_t[each] = transpose_low(projected[1, :, cols])
            values[each] = projected[2, :, cols]
            grad = attended_grad[:, cols]
            upstream[each] = grad
            product = grad.astype(jnp.float32) * attended[:, cols].astype(jnp.float32)
            inner[each] = jnp.sum(jnp.transpose(product), axis=0, keepdims=True)

    part = pl.ds(pl.multiple_of(step * block, block), block)
    queries = queries_aug[head, part, :]
    grad = upstream[head, part, :]
    scores = contract_last(keys_aug[head], queries)
    probs = jnp.exp(scores - log_totals[head, :, part])
    prob_grad = contract_last(values[head], grad)
    score_grad = (probs * (prob_grad - inner[head, :, part])).astype(jnp.bfloat16)
    value_sum[head] += jnp.dot(
        probs.astype(jnp.bfloat16), grad, preferred_element_type=jnp.float32
    )
    key_sum[head] += jnp.dot(score_grad, queries, preferred_element_type=jnp.float32)
    query_t = jnp.dot(keys_t[head], score_grad, preferred_element_type=jnp.float32)
    scale = HEAD_DIM ** (-0.5)
    query_sum[head, part, :] = jnp.transpose(query_t * scale).astype(jnp.bfloat16)

    @pl.when(jnp.logical_and(head == heads - 1, step == pl.num_programs(1) - 1))
    def _():
        every = range(heads)
        grads[0] = jnp.concatenate([query_sum[each] for each in every], axis=1)
        grads[1] = jnp.concatenate(
            [key_sum[each, :, :HEAD_DIM].astype(jnp.bfloat16) for each in every], axis=1
        )
        grads[2] = jnp.concatenate([value_sum[each].astype(jnp.bfloat16) for each in every], axis=1)


def attend_backward(scalars, projected, attended, attended_grad, log_totals):
    _, slot_rows, columns = projected.shape
    heads = columns // HEAD_DIM
    whole = pl.BlockSpec(memory_space=pltpu.VMEM)
    return pl.pallas_call(
        attend_back_kernel,
        grid_spec=pltpu.PrefetchScalarGridSpec(
            num_scalar_prefetch=1,
            grid=(heads, BACKWARD_STEPS),
            in_specs=[whole] * 4,
            out_specs=whole,
            scratch_shapes=[
                pltpu.VMEM((heads, slot_rows, 128), jnp.bfloat16),
                pltpu.VMEM((heads, slot_rows, 128), jnp.bfloat16),
                pltpu.VMEM((heads, HEAD_DIM, slot_rows), jnp.bfloat16),
                pltpu.VMEM((heads, slot_rows, HEAD_DIM), jnp.bfloat16),
                pltpu.VMEM((heads, slot_rows, HEAD_DIM), jnp.bfloat16),
                pltpu.VMEM((heads, 1, slot_rows), jnp.float32),
                pltpu.VMEM((heads, slot_rows, HEAD_DIM), jnp.bfloat16),
                pltpu.VMEM((heads, slot_rows, 128), jnp.float32),
                pltpu.VMEM((heads, slot_rows, HEAD_DIM), jnp.float32),
            ],
        ),
        out_shape=jax.ShapeDtypeStruct(projected.shape, jnp.bfloat16),
        compiler_params=pltpu.CompilerParams(vmem_limit_bytes=60 << 20),
        cost_estimate=pl.CostEstimate(
            flops=10 * heads * slot_rows * slot_rows * 256,
            bytes_accessed=8 * slot_rows * columns * 2,
            transcendentals=heads * slot_rows * slot_rows,
        ),
        name="attend_backward",
    )(scalars, projected, attended, attended_grad, log_totals)


def pair_swap(array, axis, bit):
    size = lax.axis_size(axis)
    return lax.ppermute(array, axis, [(source, source ^ bit) for source in range(size)])


def gather_relative(rows):
    across = pair_swap(rows, "tensor", 2)
    beside = pair_swap(rows, "tensor", 1)
    return (rows, beside, across, pair_swap(across, "tensor", 1))


def scatter_relative(blocks):
    low = [block.astype(jnp.bfloat16) for block in blocks]
    far = blocks[2] + pair_swap(low[3], "tensor", 1).astype(jnp.float32)
    far_low = pair_swap(far.astype(jnp.bfloat16), "tensor", 2)
    near = blocks[0] + pair_swap(low[1], "tensor", 1).astype(jnp.float32)
    return near + far_low.astype(jnp.float32)


def reduce_cells(grads, bits):
    index = lax.axis_index("dp")
    block = grads
    for bit in bits:
        half = block.shape[0] // 2
        side = (index // bit) % 2
        kept = lax.dynamic_slice_in_dim(block, side * half, half, 0)
        sent = lax.dynamic_slice_in_dim(block, (1 - side) * half, half, 0)
        got = pair_swap(sent.astype(jnp.bfloat16), "dp", bit)
        block = kept + got.astype(jnp.float32)
    block = block.astype(jnp.bfloat16)
    for bit in reversed(bits):
        side = (index // bit) % 2
        got = pair_swap(block, "dp", bit)
        block = jnp.where(
            side == 0, jnp.concatenate([block, got]), jnp.concatenate([got, block])
        )
    return block.astype(jnp.float32)


def sum_cells(grads):
    bits = [1 << step for step in range((lax.axis_size("dp") - 1).bit_length())]
    half = grads.shape[0] // 2
    rotated = bits[1:] + bits[:1]
    return jnp.concatenate([reduce_cells(grads[:half], bits), reduce_cells(grads[half:], rotated)])


def sum_small(rows, axes):
    for axis in axes:
        bit = 1
        while bit < lax.axis_size(axis):
            rows = rows + pair_swap(rows, axis, bit)
            bit *= 2
    return rows


def per_device(
    cells_x,
    cotangent,
    gene_counts,
    slot_cell,
    norm_gain,
    norm_shift,
    out_bias,
    w_qkv,
    qv_bias,
    w_out,
    w_up,
    up_bias,
    w_down,
):
    rows = cells_x.shape[0]
    width = cells_x.shape[1]
    place = lax.axis_index("tensor")
    cell_ids = jnp.arange(gene_counts.shape[0], dtype=jnp.int32)
    length = jnp.sum(jnp.where(slot_cell[0] == cell_ids, gene_counts, 0))
    positions = jnp.concatenate(
        [(place ^ block) * rows + jnp.arange(rows, dtype=jnp.int32) for block in range(4)]
    )
    live_keys = positions < length
    live_rows = live_keys[:rows]
    x_rows = jnp.concatenate(gather_relative(cells_x))
    out_grad = jnp.where(live_rows[:, None], cotangent, jnp.zeros_like(cotangent))
    grad_rows = jnp.concatenate(gather_relative(out_grad))
    normed_in, scaled_in, inverse_in = normalize(
        x_rows.astype(jnp.float32), norm_gain[0], norm_shift[0]
    )
    gathered_in = normed_in.astype(jnp.bfloat16)
    bias_rows = jnp.stack([qv_bias[0], jnp.zeros_like(qv_bias[0]), qv_bias[1]]).astype(jnp.float32)
    projected = jnp.einsum("rd,sdc->src", gathered_in, w_qkv, preferred_element_type=jnp.float32)
    projected = (projected + bias_rows[:, None, :]).astype(jnp.bfloat16)
    scalars = jnp.stack([length] + [(place ^ block) * rows for block in range(4)])
    attended_low, log_totals = attend_forward(scalars, projected)

    def cut(array):
        return [array[block * rows : (block + 1) * rows] for block in range(4)]

    attn_sum = scatter_relative(
        cut(jnp.dot(attended_low, w_out, preferred_element_type=jnp.float32))
    )
    middle = cells_x.astype(jnp.float32) + attn_sum + out_bias[0].astype(jnp.float32)
    normed_mid, scaled_mid, inverse_mid = normalize(middle, norm_gain[1], norm_shift[1])
    ffn_rows = jnp.concatenate(gather_relative(normed_mid.astype(jnp.bfloat16)))
    hidden = jnp.dot(ffn_rows, w_up, preferred_element_type=jnp.float32) + up_bias.astype(
        jnp.float32
    )
    active, gelu_back = jax.vjp(exact_gelu, hidden)
    active_low = active.astype(jnp.bfloat16)
    hidden_grad = gelu_back(contract_last(grad_rows, w_down))[0].astype(jnp.bfloat16)
    mid_norm_grad = scatter_relative(cut(contract_last(hidden_grad, w_up)))
    branch = scatter_relative(cut(jnp.dot(active_low, w_down, preferred_element_type=jnp.float32)))
    output = jnp.where(live_rows[:, None], middle + branch + out_bias[1].astype(jnp.float32), 0.0)
    block_out = output.astype(jnp.bfloat16)
    down_grad = contract_first(active_low, grad_rows)
    up_grad = contract_first(ffn_rows, hidden_grad)
    up_bias_grad = jnp.sum(hidden_grad, axis=0, dtype=jnp.float32)
    mid_back, gain_mid, shift_mid = normalize_back(
        mid_norm_grad, scaled_mid, inverse_mid, norm_gain[1]
    )
    middle_grad = out_grad.astype(jnp.float32) + mid_back
    middle_rows = jnp.concatenate(gather_relative(middle_grad.astype(jnp.bfloat16)))
    ffn_grads = sum_cells(jnp.concatenate([up_grad, down_grad]))
    up_grad, down_grad = ffn_grads[: up_grad.shape[0]], ffn_grads[up_grad.shape[0] :]
    attended_grad = contract_last(middle_rows, w_out).astype(jnp.bfloat16)
    out_weight_grad = contract_first(attended_low, middle_rows)
    qkv_grad = attend_backward(scalars, projected, attended_low, attended_grad, log_totals)
    in_norm_part = jnp.einsum("src,sdc->rd", qkv_grad, w_qkv, preferred_element_type=jnp.float32)
    in_norm_grad = scatter_relative(cut(in_norm_part))
    qkv_weight_grad = jnp.einsum(
        "rd,src->sdc", gathered_in, qkv_grad, preferred_element_type=jnp.float32
    )
    query_bias = jnp.sum(qkv_grad[0], axis=0, dtype=jnp.float32)
    value_bias = jnp.sum(qkv_grad[2], axis=0, dtype=jnp.float32)
    own = slice(0, rows)
    in_back, _, _ = normalize_back(in_norm_grad, scaled_in[own], inverse_in[own], norm_gain[0])
    input_grad = (middle_grad + in_back).astype(jnp.bfloat16)
    shared = sum_small(
        jnp.stack(
            [
                jnp.sum(in_norm_part * scaled_in, axis=0),
                gain_mid,
                jnp.sum(in_norm_part, axis=0),
                shift_mid,
                jnp.sum(middle_grad, axis=0),
                jnp.sum(out_grad, axis=0, dtype=jnp.float32),
            ]
        ),
        ("tensor", "dp"),
    )
    sharded = sum_small(jnp.concatenate([up_bias_grad, query_bias, value_bias])[None], ("dp",))[0]
    columns = w_qkv.shape[2]
    attn_grads = sum_cells(
        jnp.concatenate([out_weight_grad, qkv_weight_grad.reshape(-1, width)])
    )
    out_weight_grad = attn_grads[:columns]
    qkv_weight_grad = attn_grads[columns:].reshape(w_qkv.shape)
    units = up_bias.shape[0]
    return (
        block_out,
        input_grad,
        shared[0:2],
        shared[2:4],
        shared[4:6],
        qkv_weight_grad,
        sharded[units:].reshape(2, columns),
        out_weight_grad,
        up_grad,
        sharded[:units],
        down_grad,
    )


def solution(mesh):
    return jax.shard_map(
        per_device,
        mesh=mesh,
        in_specs=(
            P(("dp", "tensor"), None),
            P(("dp", "tensor"), None),
            P(),
            P("dp"),
            P(),
            P(),
            P(),
            P(None, None, "tensor"),
            P(None, "tensor"),
            P("tensor", None),
            P(None, "tensor"),
            P("tensor"),
            P("tensor", None),
        ),
        out_specs=(
            P(("dp", "tensor"), None),
            P(("dp", "tensor"), None),
            P(),
            P(),
            P(),
            P(None, None, "tensor"),
            P(None, "tensor"),
            P("tensor", None),
            P(None, "tensor"),
            P("tensor"),
            P("tensor", None),
        ),
        check_vma=False,
    )
```

```python
import jax
import jax.numpy as jnp
from jax import lax
from jax.experimental import pallas as pl
from jax.experimental.pallas import tpu as pltpu
from jax.sharding import PartitionSpec as P

HEAD_DIM = 64
SLOT = 2048


EPSILON = 1e-05
NEGATIVE = -1e30
FORWARD_STEPS = 4
BACKWARD_STEPS = 4


def exact_gelu(hidden):
    return jax.nn.gelu(hidden, approximate=False)


def normalize(features, gain_row, shift_row):
    row_mean = jnp.mean(features, axis=-1, keepdims=True)
    centered = features - row_mean
    variance = jnp.mean(centered * centered, axis=-1, keepdims=True)
    inverse = lax.rsqrt(variance + EPSILON)
    scaled = centered * inverse
    return (scaled * gain_row.astype(jnp.float32) + shift_row.astype(jnp.float32), scaled, inverse)


def normalize_back(upstream, scaled, inverse, gain_row):
    graded = upstream * gain_row.astype(jnp.float32)
    grad_mean = jnp.mean(graded, axis=-1, keepdims=True)
    cross_mean = jnp.mean(graded * scaled, axis=-1, keepdims=True)
    return (
        inverse * (graded - grad_mean - scaled * cross_mean),
        jnp.sum(upstream * scaled, axis=0),
        jnp.sum(upstream, axis=0),
    )


def contract_last(left, right):
    return lax.dot_general(
        left, right, (((1,), (1,)), ((), ())), preferred_element_type=jnp.float32
    )


def contract_first(left, right):
    return lax.dot_general(
        left, right, (((0,), (0,)), ((), ())), preferred_element_type=jnp.float32
    )


def transpose_low(array):
    return jnp.transpose(array.astype(jnp.float32)).astype(jnp.bfloat16)


def fill_heads(scalars, projected, keys_aug, queries_aug):
    heads, slot_rows, _ = keys_aug.shape
    rows = slot_rows // 4
    scale = HEAD_DIM ** (-0.5)
    column = lax.broadcasted_iota(jnp.int32, (rows, HEAD_DIM), 1)
    row = lax.broadcasted_iota(jnp.int32, (rows, HEAD_DIM), 0)
    ones = jnp.where(column == 0, 1.0, 0.0).astype(jnp.bfloat16)
    for block in range(4):
        part = pl.ds(block * rows, rows)
        dead = (scalars[1 + block] + row) >= scalars[0]
        bias = jnp.where(jnp.logical_and(dead, column == 0), NEGATIVE, 0.0).astype(jnp.bfloat16)
        queries = (projected[0, part, :].astype(jnp.float32) * scale).astype(jnp.bfloat16)
        keys = projected[1, part, :]
        for head in range(heads):
            cols = slice(head * HEAD_DIM, (head + 1) * HEAD_DIM)
            queries_aug[head, part, :] = jnp.concatenate([queries[:, cols], ones], axis=1)
            keys_aug[head, part, :] = jnp.concatenate([keys[:, cols], bias], axis=1)


def attend_kernel(
    scalars, projected, attended, log_totals, keys_aug, queries_aug, values_t, result
):
    head, step = pl.program_id(0), pl.program_id(1)
    heads, slot_rows, _ = keys_aug.shape
    block = slot_rows // pl.num_programs(1)

    @pl.when(jnp.logical_and(head == 0, step == 0))
    def _():
        fill_heads(scalars, projected, keys_aug, queries_aug)
        extra = lax.broadcasted_iota(jnp.int32, (16, slot_rows), 0)
        ones = jnp.where(extra == 0, 1.0, 0.0).astype(jnp.bfloat16)
        for each in range(heads):
            cols = slice(each * HEAD_DIM, (each + 1) * HEAD_DIM)
            values_t[each, :HEAD_DIM, :] = transpose_low(projected[2, :, cols])
            values_t[each, HEAD_DIM:, :] = ones

    part = pl.ds(pl.multiple_of(step * block, block), block)
    scores = contract_last(keys_aug[head], queries_aug[head, part, :])
    row_max = jnp.max(scores, axis=0, keepdims=True)
    probs = jnp.exp(scores - row_max).astype(jnp.bfloat16)
    mixed = jnp.dot(values_t[head], probs, preferred_element_type=jnp.float32)
    total = mixed[HEAD_DIM : HEAD_DIM + 1, :]
    result[head, part, :] = jnp.transpose(mixed[:HEAD_DIM, :] / total).astype(jnp.bfloat16)
    log_totals[head, :, part] = row_max + jnp.log(total)

    @pl.when(jnp.logical_and(head == heads - 1, step == pl.num_programs(1) - 1))
    def _():
        attended[...] = jnp.concatenate([result[each] for each in range(heads)], axis=1)


def attend_forward(scalars, projected):
    _, slot_rows, columns = projected.shape
    heads = columns // HEAD_DIM
    whole = pl.BlockSpec(memory_space=pltpu.VMEM)
    return pl.pallas_call(
        attend_kernel,
        grid_spec=pltpu.PrefetchScalarGridSpec(
            num_scalar_prefetch=1,
            grid=(heads, FORWARD_STEPS),
            in_specs=[whole],
            out_specs=[whole, whole],
            scratch_shapes=[
                pltpu.VMEM((heads, slot_rows, 128), jnp.bfloat16),
                pltpu.VMEM((heads, slot_rows, 128), jnp.bfloat16),
                pltpu.VMEM((heads, HEAD_DIM + 16, slot_rows), jnp.bfloat16),
                pltpu.VMEM((heads, slot_rows, HEAD_DIM), jnp.bfloat16),
            ],
        ),
        out_shape=[
            jax.ShapeDtypeStruct((slot_rows, columns), jnp.bfloat16),
            jax.ShapeDtypeStruct((heads, 1, slot_rows), jnp.float32),
        ],
        compiler_params=pltpu.CompilerParams(vmem_limit_bytes=60 << 20),
        cost_estimate=pl.CostEstimate(
            flops=4 * heads * slot_rows * slot_rows * 256,
            bytes_accessed=5 * slot_rows * columns * 2,
            transcendentals=heads * slot_rows * slot_rows,
        ),
        name="attend_forward",
    )(scalars, projected)


def attend_back_kernel(
    scalars,
    projected,
    attended,
    attended_grad,
    log_totals,
    grads,
    keys_aug,
    queries_aug,
    keys_t,
    values,
    upstream,
    inner,
    query_sum,
    key_sum,
    value_sum,
):
    head, step = pl.program_id(0), pl.program_id(1)
    heads, slot_rows, _ = keys_aug.shape
    block = slot_rows // pl.num_programs(1)

    @pl.when(jnp.logical_and(head == 0, step == 0))
    def _():
        fill_heads(scalars, projected, keys_aug, queries_aug)
        key_sum[...] = jnp.zeros_like(key_sum)
        value_sum[...] = jnp.zeros_like(value_sum)
        for each in range(heads):
            cols = slice(each * HEAD_DIM, (each + 1) * HEAD_DIM)
            keys_t[each] = transpose_low(projected[1, :, cols])
            values[each] = projected[2, :, cols]
            grad = attended_grad[:, cols]
            upstream[each] = grad
            product = grad.astype(jnp.float32) * attended[:, cols].astype(jnp.float32)
            inner[each] = jnp.sum(jnp.transpose(product), axis=0, keepdims=True)

    part = pl.ds(pl.multiple_of(step * block, block), block)
    queries = queries_aug[head, part, :]
    grad = upstream[head, part, :]
    scores = contract_last(keys_aug[head], queries)
    probs = jnp.exp(scores - log_totals[head, :, part])
    prob_grad = contract_last(values[head], grad)
    score_grad = (probs * (prob_grad - inner[head, :, part])).astype(jnp.bfloat16)
    value_sum[head] += jnp.dot(
        probs.astype(jnp.bfloat16), grad, preferred_element_type=jnp.float32
    )
    key_sum[head] += jnp.dot(score_grad, queries, preferred_element_type=jnp.float32)
    query_t = jnp.dot(keys_t[head], score_grad, preferred_element_type=jnp.float32)
    scale = HEAD_DIM ** (-0.5)
    query_sum[head, part, :] = jnp.transpose(query_t * scale).astype(jnp.bfloat16)

    @pl.when(jnp.logical_and(head == heads - 1, step == pl.num_programs(1) - 1))
    def _():
        every = range(heads)
        grads[0] = jnp.concatenate([query_sum[each] for each in every], axis=1)
        grads[1] = jnp.concatenate(
            [key_sum[each, :, :HEAD_DIM].astype(jnp.bfloat16) for each in every], axis=1
        )
        grads[2] = jnp.concatenate([value_sum[each].astype(jnp.bfloat16) for each in every], axis=1)


def attend_backward(scalars, projected, attended, attended_grad, log_totals):
    _, slot_rows, columns = projected.shape
    heads = columns // HEAD_DIM
    whole = pl.BlockSpec(memory_space=pltpu.VMEM)
    return pl.pallas_call(
        attend_back_kernel,
        grid_spec=pltpu.PrefetchScalarGridSpec(
            num_scalar_prefetch=1,
            grid=(heads, BACKWARD_STEPS),
            in_specs=[whole] * 4,
            out_specs=whole,
            scratch_shapes=[
                pltpu.VMEM((heads, slot_rows, 128), jnp.bfloat16),
                pltpu.VMEM((heads, slot_rows, 128), jnp.bfloat16),
                pltpu.VMEM((heads, HEAD_DIM, slot_rows), jnp.bfloat16),
                pltpu.VMEM((heads, slot_rows, HEAD_DIM), jnp.bfloat16),
                pltpu.VMEM((heads, slot_rows, HEAD_DIM), jnp.bfloat16),
                pltpu.VMEM((heads, 1, slot_rows), jnp.float32),
                pltpu.VMEM((heads, slot_rows, HEAD_DIM), jnp.bfloat16),
                pltpu.VMEM((heads, slot_rows, 128), jnp.float32),
                pltpu.VMEM((heads, slot_rows, HEAD_DIM), jnp.float32),
            ],
        ),
        out_shape=jax.ShapeDtypeStruct(projected.shape, jnp.bfloat16),
        compiler_params=pltpu.CompilerParams(vmem_limit_bytes=60 << 20),
        cost_estimate=pl.CostEstimate(
            flops=10 * heads * slot_rows * slot_rows * 256,
            bytes_accessed=8 * slot_rows * columns * 2,
            transcendentals=heads * slot_rows * slot_rows,
        ),
        name="attend_backward",
    )(scalars, projected, attended, attended_grad, log_totals)


def normed(features):
    row_mean = jnp.mean(features, axis=-1, keepdims=True)
    centered = features - row_mean
    variance = jnp.mean(centered * centered, axis=-1, keepdims=True)
    return centered * lax.rsqrt(variance + EPSILON)


def project_kernel(features, norms, weights, biases, *refs):
    normed_rows, projected = refs[-2:]
    scaled = normed(features[...].astype(jnp.float32))
    low = (scaled * norms[0:1, :] + norms[1:2, :]).astype(jnp.bfloat16)
    normed_rows[...] = low
    for part in range(3):
        product = jnp.dot(low, weights[part], preferred_element_type=jnp.float32)
        projected[part] = (product + biases[part : part + 1, :]).astype(jnp.bfloat16)


def project_rows(features, norms, weights, biases, block, earlier):
    rows, width = features.shape
    columns = weights.shape[2]
    whole = pl.BlockSpec(memory_space=pltpu.VMEM)
    place = pl.BlockSpec(memory_space=pl.ANY)
    return pl.pallas_call(
        project_kernel,
        grid=(1,),
        in_specs=[whole] * 4 + [place] * len(earlier),
        out_specs=[
            pl.BlockSpec((rows, width), lambda step: (block, 0)),
            pl.BlockSpec((3, rows, columns), lambda step: (0, block, 0)),
        ],
        out_shape=[
            jax.ShapeDtypeStruct((4 * rows, width), jnp.bfloat16),
            jax.ShapeDtypeStruct((3, 4 * rows, columns), jnp.bfloat16),
        ],
        input_output_aliases={4 + index: index for index in range(len(earlier))},
        compiler_params=pltpu.CompilerParams(vmem_limit_bytes=32 << 20),
        cost_estimate=pl.CostEstimate(
            flops=6 * rows * width * columns,
            bytes_accessed=4 * rows * width + 6 * (rows + width) * columns,
            transcendentals=0,
        ),
        name="project_rows",
    )(features, norms, weights, biases, *earlier)


def input_back_kernel(own, beside, across, far, grads, weights, near, low, sums, features):
    step = pl.program_id(0)
    for index, piece in enumerate((own, beside, across, far)):

        @pl.when(step == index)
        def _():
            features[...] = piece[...]

    rows = own.shape[0]
    part = pl.ds(pl.multiple_of(step * rows, rows), rows)
    product = contract_last(grads[0, part, :], weights[0])
    for index in (1, 2):
        product += contract_last(grads[index, part, :], weights[index])

    @pl.when(step % 2 == 0)
    def _():
        near[step // 2] = product

    @pl.when(step % 2 == 1)
    def _():
        low[step // 2] = product.astype(jnp.bfloat16)

    @pl.when(step == 0)
    def _():
        sums[...] = jnp.zeros_like(sums)

    scaled = normed(features[...].astype(jnp.float32))
    sums[0:1, :] += jnp.sum(product * scaled, axis=0, keepdims=True)
    sums[1:2, :] += jnp.sum(product, axis=0, keepdims=True)


def input_back(pieces, grads, weights):
    rows, width = pieces[0].shape
    columns = weights.shape[2]
    whole = pl.BlockSpec(memory_space=pltpu.VMEM)
    return pl.pallas_call(
        input_back_kernel,
        grid=(4,),
        in_specs=[whole] * 6,
        out_specs=[whole] * 3,
        out_shape=[
            jax.ShapeDtypeStruct((2, rows, width), jnp.float32),
            jax.ShapeDtypeStruct((2, rows, width), jnp.bfloat16),
            jax.ShapeDtypeStruct((8, width), jnp.float32),
        ],
        scratch_shapes=[pltpu.VMEM((rows, width), jnp.bfloat16)],
        compiler_params=pltpu.CompilerParams(vmem_limit_bytes=48 << 20),
        cost_estimate=pl.CostEstimate(
            flops=24 * rows * width * columns,
            bytes_accessed=20 * rows * width + 6 * (4 * rows + width) * columns,
            transcendentals=0,
        ),
        name="input_back",
    )(*pieces, grads, weights)


def pair_swap(array, axis, bit):
    size = lax.axis_size(axis)
    return lax.ppermute(array, axis, [(source, source ^ bit) for source in range(size)])


def gather_relative(rows):
    across = pair_swap(rows, "tensor", 2)
    beside = pair_swap(rows, "tensor", 1)
    return (rows, beside, across, pair_swap(across, "tensor", 1))


def finish_scatter(own, beside_low, across, far_low):
    across = across + pair_swap(far_low, "tensor", 1).astype(jnp.float32)
    got = pair_swap(across.astype(jnp.bfloat16), "tensor", 2)
    own = own + pair_swap(beside_low, "tensor", 1).astype(jnp.float32)
    return own + got.astype(jnp.float32)


def scatter_relative(blocks):
    return finish_scatter(
        blocks[0], blocks[1].astype(jnp.bfloat16), blocks[2], blocks[3].astype(jnp.bfloat16)
    )


def reduce_cells(grads, bits):
    index = lax.axis_index("dp")
    block = grads
    for bit in bits:
        half = block.shape[0] // 2
        side = (index // bit) % 2
        kept = lax.dynamic_slice_in_dim(block, side * half, half, 0)
        sent = lax.dynamic_slice_in_dim(block, (1 - side) * half, half, 0)
        got = pair_swap(sent.astype(jnp.bfloat16), "dp", bit)
        block = kept + got.astype(jnp.float32)
    block = block.astype(jnp.bfloat16)
    for bit in reversed(bits):
        side = (index // bit) % 2
        got = pair_swap(block, "dp", bit)
        block = jnp.where(
            side == 0, jnp.concatenate([block, got]), jnp.concatenate([got, block])
        )
    return block.astype(jnp.float32)


def sum_cells(grads):
    bits = [1 << step for step in range((lax.axis_size("dp") - 1).bit_length())]
    half = grads.shape[0] // 2
    rotated = bits[1:] + bits[:1]
    return jnp.concatenate([reduce_cells(grads[:half], bits), reduce_cells(grads[half:], rotated)])


def sum_small(rows, axes):
    for axis in axes:
        bit = 1
        while bit < lax.axis_size(axis):
            rows = rows + pair_swap(rows, axis, bit)
            bit *= 2
    return rows


def per_device(
    cells_x,
    cotangent,
    gene_counts,
    slot_cell,
    norm_gain,
    norm_shift,
    out_bias,
    w_qkv,
    qv_bias,
    w_out,
    w_up,
    up_bias,
    w_down,
):
    rows = cells_x.shape[0]
    width = cells_x.shape[1]
    place = lax.axis_index("tensor")
    cell_ids = jnp.arange(gene_counts.shape[0], dtype=jnp.int32)
    length = jnp.sum(jnp.where(slot_cell[0] == cell_ids, gene_counts, 0))
    positions = jnp.concatenate(
        [(place ^ block) * rows + jnp.arange(rows, dtype=jnp.int32) for block in range(4)]
    )
    live_keys = positions < length
    live_rows = live_keys[:rows]
    pieces = gather_relative(cells_x)
    out_grad = jnp.where(live_rows[:, None], cotangent, jnp.zeros_like(cotangent))
    late_grad, _ = lax.optimization_barrier((out_grad, pieces[2]))
    grad_pieces = gather_relative(late_grad)
    norms_in = jnp.stack([norm_gain[0], norm_shift[0]]).astype(jnp.float32)
    biases = jnp.stack([qv_bias[0], jnp.zeros_like(qv_bias[0]), qv_bias[1]]).astype(jnp.float32)
    buffers = ()
    for block in range(4):
        buffers = project_rows(pieces[block], norms_in, w_qkv, biases, block, buffers)
    gathered_in, projected = buffers
    scalars = jnp.stack([length] + [(place ^ block) * rows for block in range(4)])
    attended_low, log_totals = attend_forward(scalars, projected)
    (attended_low, log_totals), grad_pieces = lax.optimization_barrier(
        ((attended_low, log_totals), grad_pieces)
    )
    grad_rows = jnp.concatenate(grad_pieces)

    def cut(array):
        return [array[block * rows : (block + 1) * rows] for block in range(4)]

    attn_sum = scatter_relative(
        cut(jnp.dot(attended_low, w_out, preferred_element_type=jnp.float32))
    )
    middle = cells_x.astype(jnp.float32) + attn_sum + out_bias[0].astype(jnp.float32)
    normed_mid, scaled_mid, inverse_mid = normalize(middle, norm_gain[1], norm_shift[1])
    ffn_rows = jnp.concatenate(gather_relative(normed_mid.astype(jnp.bfloat16)))
    hidden = jnp.dot(ffn_rows, w_up, preferred_element_type=jnp.float32) + up_bias.astype(
        jnp.float32
    )
    active, gelu_back = jax.vjp(exact_gelu, hidden)
    active_low = active.astype(jnp.bfloat16)
    hidden_grad = gelu_back(contract_last(grad_rows, w_down))[0].astype(jnp.bfloat16)
    mid_norm_grad = scatter_relative(cut(contract_last(hidden_grad, w_up)))
    branch = scatter_relative(cut(jnp.dot(active_low, w_down, preferred_element_type=jnp.float32)))
    output = jnp.where(live_rows[:, None], middle + branch + out_bias[1].astype(jnp.float32), 0.0)
    block_out = output.astype(jnp.bfloat16)
    down_grad = contract_first(active_low, grad_rows)
    up_grad = contract_first(ffn_rows, hidden_grad)
    up_bias_grad = jnp.sum(hidden_grad, axis=0, dtype=jnp.float32)
    mid_back, gain_mid, shift_mid = normalize_back(
        mid_norm_grad, scaled_mid, inverse_mid, norm_gain[1]
    )
    middle_grad = out_grad.astype(jnp.float32) + mid_back
    middle_rows = jnp.concatenate(gather_relative(middle_grad.astype(jnp.bfloat16)))
    ffn_grads = lax.psum(jnp.concatenate([up_grad, down_grad]).astype(jnp.bfloat16), "dp")
    ffn_grads = ffn_grads.astype(jnp.float32)
    up_grad, down_grad = ffn_grads[: up_grad.shape[0]], ffn_grads[up_grad.shape[0] :]
    attended_grad = contract_last(middle_rows, w_out).astype(jnp.bfloat16)
    out_weight_grad = contract_first(attended_low, middle_rows)
    qkv_grad = attend_backward(scalars, projected, attended_low, attended_grad, log_totals)
    near, low, sums = input_back(pieces, qkv_grad, w_qkv)
    in_norm_grad = finish_scatter(near[0], low[0], near[1], low[1])
    qkv_weight_grad = jnp.einsum(
        "rd,src->scd", gathered_in, qkv_grad, preferred_element_type=jnp.float32
    )
    query_bias = jnp.sum(qkv_grad[0], axis=0, dtype=jnp.float32)
    value_bias = jnp.sum(qkv_grad[2], axis=0, dtype=jnp.float32)
    _, scaled_in, inverse_in = normalize(
        cells_x.astype(jnp.float32), norm_gain[0], norm_shift[0]
    )
    in_back, _, _ = normalize_back(in_norm_grad, scaled_in, inverse_in, norm_gain[0])
    input_grad = (middle_grad + in_back).astype(jnp.bfloat16)
    shared = sum_small(
        jnp.stack(
            [
                sums[0],
                gain_mid,
                sums[1],
                shift_mid,
                jnp.sum(middle_grad, axis=0),
                jnp.sum(out_grad, axis=0, dtype=jnp.float32),
            ]
        ),
        ("tensor",),
    )
    columns = w_qkv.shape[2]
    units = up_bias.shape[0]
    heavy = jnp.concatenate([out_weight_grad, qkv_weight_grad.reshape(-1, width)])
    light = jnp.concatenate([up_bias_grad, query_bias, value_bias])
    light_rows = -(-light.shape[0] // width)
    light = jnp.pad(light, (0, light_rows * width - light.shape[0])).reshape(light_rows, width)
    payload = jnp.concatenate([heavy, shared, light])
    filled = payload.shape[0]
    payload = sum_cells(jnp.pad(payload, ((0, -filled % 128), (0, 0))))
    first = heavy.shape[0]
    shared = payload[first : first + 6]
    sharded = payload[first + 6 : filled].reshape(-1)
    out_weight_grad = payload[:columns]
    qkv_weight_grad = jnp.swapaxes(payload[columns:first].reshape(3, columns, width), 1, 2)
    return (
        block_out,
        input_grad,
        shared[0:2],
        shared[2:4],
        shared[4:6],
        qkv_weight_grad,
        sharded[units : units + 2 * columns].reshape(2, columns),
        out_weight_grad,
        up_grad,
        sharded[:units],
        down_grad,
    )


def solution(mesh):
    return jax.shard_map(
        per_device,
        mesh=mesh,
        in_specs=(
            P(("dp", "tensor"), None),
            P(("dp", "tensor"), None),
            P(),
            P("dp"),
            P(),
            P(),
            P(),
            P(None, None, "tensor"),
            P(None, "tensor"),
            P("tensor", None),
            P(None, "tensor"),
            P("tensor"),
            P("tensor", None),
        ),
        out_specs=(
            P(("dp", "tensor"), None),
            P(("dp", "tensor"), None),
            P(),
            P(),
            P(),
            P(None, None, "tensor"),
            P(None, "tensor"),
            P("tensor", None),
            P(None, "tensor"),
            P("tensor"),
            P("tensor", None),
        ),
        check_vma=False,
    )
```

```python
import functools

import jax
import jax.numpy as jnp
from jax import lax
from jax.experimental import pallas as pl
from jax.experimental.pallas import tpu as pltpu
from jax.sharding import PartitionSpec as P


HEAD_DIM = 64


EPSILON = 1e-05
NEGATIVE = -1e30
FORWARD_STEPS = 4
BACKWARD_STEPS = 4
FEED_TILE = 256


def normalize(features, gain_row, shift_row):
    row_mean = jnp.mean(features, axis=-1, keepdims=True)
    centered = features - row_mean
    variance = jnp.mean(centered * centered, axis=-1, keepdims=True)
    inverse = lax.rsqrt(variance + EPSILON)
    scaled = centered * inverse
    return (scaled * gain_row.astype(jnp.float32) + shift_row.astype(jnp.float32), scaled, inverse)


def normalize_back(upstream, scaled, inverse, gain_row):
    graded = upstream * gain_row.astype(jnp.float32)
    grad_mean = jnp.mean(graded, axis=-1, keepdims=True)
    cross_mean = jnp.mean(graded * scaled, axis=-1, keepdims=True)
    return (
        inverse * (graded - grad_mean - scaled * cross_mean),
        jnp.sum(upstream * scaled, axis=0),
        jnp.sum(upstream, axis=0),
    )


def contract_last(left, right):
    return lax.dot_general(
        left, right, (((1,), (1,)), ((), ())), preferred_element_type=jnp.float32
    )


def contract_first(left, right):
    return lax.dot_general(
        left, right, (((0,), (0,)), ((), ())), preferred_element_type=jnp.float32
    )


def transpose_low(array):
    return jnp.transpose(array.astype(jnp.float32)).astype(jnp.bfloat16)


def fill_heads(scalars, projected, keys_aug, queries_aug):
    heads, slot_rows, _ = keys_aug.shape
    rows = slot_rows // 4
    scale = HEAD_DIM ** (-0.5)
    column = lax.broadcasted_iota(jnp.int32, (rows, HEAD_DIM), 1)
    row = lax.broadcasted_iota(jnp.int32, (rows, HEAD_DIM), 0)
    ones = jnp.where(column == 0, 1.0, 0.0).astype(jnp.bfloat16)
    for block in range(4):
        part = pl.ds(block * rows, rows)
        dead = (scalars[1 + block] + row) >= scalars[0]
        bias = jnp.where(jnp.logical_and(dead, column == 0), NEGATIVE, 0.0).astype(jnp.bfloat16)
        queries = (projected[0, part, :].astype(jnp.float32) * scale).astype(jnp.bfloat16)
        keys = projected[1, part, :]
        for head in range(heads):
            cols = slice(head * HEAD_DIM, (head + 1) * HEAD_DIM)
            queries_aug[head, part, :] = jnp.concatenate([queries[:, cols], ones], axis=1)
            keys_aug[head, part, :] = jnp.concatenate([keys[:, cols], bias], axis=1)


def attend_kernel(
    scalars, projected, attended, log_totals, keys_aug, queries_aug, values_t, result
):
    head, step = pl.program_id(0), pl.program_id(1)
    heads, slot_rows, _ = keys_aug.shape
    block = slot_rows // pl.num_programs(1)

    @pl.when(jnp.logical_and(head == 0, step == 0))
    def _():
        fill_heads(scalars, projected, keys_aug, queries_aug)
        extra = lax.broadcasted_iota(jnp.int32, (16, slot_rows), 0)
        ones = jnp.where(extra == 0, 1.0, 0.0).astype(jnp.bfloat16)
        for each in range(heads):
            cols = slice(each * HEAD_DIM, (each + 1) * HEAD_DIM)
            values_t[each, :HEAD_DIM, :] = transpose_low(projected[2, :, cols])
            values_t[each, HEAD_DIM:, :] = ones

    part = pl.ds(pl.multiple_of(step * block, block), block)
    scores = contract_last(keys_aug[head], queries_aug[head, part, :])
    row_max = jnp.max(scores, axis=0, keepdims=True)
    probs = jnp.exp(scores - row_max).astype(jnp.bfloat16)
    mixed = jnp.dot(values_t[head], probs, preferred_element_type=jnp.float32)
    total = mixed[HEAD_DIM : HEAD_DIM + 1, :]
    result[head, part, :] = jnp.transpose(mixed[:HEAD_DIM, :] / total).astype(jnp.bfloat16)
    log_totals[head, :, part] = row_max + jnp.log(total)

    @pl.when(jnp.logical_and(head == heads - 1, step == pl.num_programs(1) - 1))
    def _():
        attended[...] = jnp.concatenate([result[each] for each in range(heads)], axis=1)


def attend_forward(scalars, projected):
    _, slot_rows, columns = projected.shape
    heads = columns // HEAD_DIM
    whole = pl.BlockSpec(memory_space=pltpu.VMEM)
    return pl.pallas_call(
        attend_kernel,
        grid_spec=pltpu.PrefetchScalarGridSpec(
            num_scalar_prefetch=1,
            grid=(heads, FORWARD_STEPS),
            in_specs=[whole],
            out_specs=[whole, whole],
            scratch_shapes=[
                pltpu.VMEM((heads, slot_rows, 128), jnp.bfloat16),
                pltpu.VMEM((heads, slot_rows, 128), jnp.bfloat16),
                pltpu.VMEM((heads, HEAD_DIM + 16, slot_rows), jnp.bfloat16),
                pltpu.VMEM((heads, slot_rows, HEAD_DIM), jnp.bfloat16),
            ],
        ),
        out_shape=[
            jax.ShapeDtypeStruct((slot_rows, columns), jnp.bfloat16),
            jax.ShapeDtypeStruct((heads, 1, slot_rows), jnp.float32),
        ],
        compiler_params=pltpu.CompilerParams(vmem_limit_bytes=60 << 20),
        cost_estimate=pl.CostEstimate(
            flops=4 * heads * slot_rows * slot_rows * 256,
            bytes_accessed=5 * slot_rows * columns * 2,
            transcendentals=heads * slot_rows * slot_rows,
        ),
        name="attend_forward",
    )(scalars, projected)


def attend_back_kernel(
    scalars,
    projected,
    attended,
    attended_grad,
    log_totals,
    grads,
    keys_aug,
    queries_aug,
    keys_t,
    values,
    upstream,
    inner,
    query_sum,
    key_sum,
    value_sum,
):
    head, step = pl.program_id(0), pl.program_id(1)
    heads, slot_rows, _ = keys_aug.shape
    block = slot_rows // pl.num_programs(1)

    @pl.when(jnp.logical_and(head == 0, step == 0))
    def _():
        fill_heads(scalars, projected, keys_aug, queries_aug)
        key_sum[...] = jnp.zeros_like(key_sum)
        value_sum[...] = jnp.zeros_like(value_sum)
        for each in range(heads):
            cols = slice(each * HEAD_DIM, (each + 1) * HEAD_DIM)
            keys_t[each] = transpose_low(projected[1, :, cols])
            values[each] = projected[2, :, cols]
            grad = attended_grad[:, cols]
            upstream[each] = grad
            product = grad.astype(jnp.float32) * attended[:, cols].astype(jnp.float32)
            inner[each] = jnp.sum(jnp.transpose(product), axis=0, keepdims=True)

    part = pl.ds(pl.multiple_of(step * block, block), block)
    queries = queries_aug[head, part, :]
    grad = upstream[head, part, :]
    scores = contract_last(keys_aug[head], queries)
    probs = jnp.exp(scores - log_totals[head, :, part])
    prob_grad = contract_last(values[head], grad)
    score_grad = (probs * (prob_grad - inner[head, :, part])).astype(jnp.bfloat16)
    value_sum[head] += jnp.dot(
        probs.astype(jnp.bfloat16), grad, preferred_element_type=jnp.float32
    )
    key_sum[head] += jnp.dot(score_grad, queries, preferred_element_type=jnp.float32)
    query_t = jnp.dot(keys_t[head], score_grad, preferred_element_type=jnp.float32)
    scale = HEAD_DIM ** (-0.5)
    query_sum[head, part, :] = jnp.transpose(query_t * scale).astype(jnp.bfloat16)

    @pl.when(jnp.logical_and(head == heads - 1, step == pl.num_programs(1) - 1))
    def _():
        every = range(heads)
        grads[0] = jnp.concatenate([query_sum[each] for each in every], axis=1)
        grads[1] = jnp.concatenate(
            [key_sum[each, :, :HEAD_DIM].astype(jnp.bfloat16) for each in every], axis=1
        )
        grads[2] = jnp.concatenate([value_sum[each].astype(jnp.bfloat16) for each in every], axis=1)


def attend_backward(scalars, projected, attended, attended_grad, log_totals):
    _, slot_rows, columns = projected.shape
    heads = columns // HEAD_DIM
    whole = pl.BlockSpec(memory_space=pltpu.VMEM)
    return pl.pallas_call(
        attend_back_kernel,
        grid_spec=pltpu.PrefetchScalarGridSpec(
            num_scalar_prefetch=1,
            grid=(heads, BACKWARD_STEPS),
            in_specs=[whole] * 4,
            out_specs=whole,
            scratch_shapes=[
                pltpu.VMEM((heads, slot_rows, 128), jnp.bfloat16),
                pltpu.VMEM((heads, slot_rows, 128), jnp.bfloat16),
                pltpu.VMEM((heads, HEAD_DIM, slot_rows), jnp.bfloat16),
                pltpu.VMEM((heads, slot_rows, HEAD_DIM), jnp.bfloat16),
                pltpu.VMEM((heads, slot_rows, HEAD_DIM), jnp.bfloat16),
                pltpu.VMEM((heads, 1, slot_rows), jnp.float32),
                pltpu.VMEM((heads, slot_rows, HEAD_DIM), jnp.bfloat16),
                pltpu.VMEM((heads, slot_rows, 128), jnp.float32),
                pltpu.VMEM((heads, slot_rows, HEAD_DIM), jnp.float32),
            ],
        ),
        out_shape=jax.ShapeDtypeStruct(projected.shape, jnp.bfloat16),
        compiler_params=pltpu.CompilerParams(vmem_limit_bytes=60 << 20),
        cost_estimate=pl.CostEstimate(
            flops=10 * heads * slot_rows * slot_rows * 256,
            bytes_accessed=8 * slot_rows * columns * 2,
            transcendentals=heads * slot_rows * slot_rows,
        ),
        name="attend_backward",
    )(scalars, projected, attended, attended_grad, log_totals)


def normed(features):
    row_mean = jnp.mean(features, axis=-1, keepdims=True)
    centered = features - row_mean
    variance = jnp.mean(centered * centered, axis=-1, keepdims=True)
    return centered * lax.rsqrt(variance + EPSILON)


def project_kernel(features, norms, weights, biases, *refs):
    normed_rows, projected = refs[-2:]
    scaled = normed(features[...].astype(jnp.float32))
    low = (scaled * norms[0:1, :] + norms[1:2, :]).astype(jnp.bfloat16)
    normed_rows[...] = low
    for part in range(3):
        product = jnp.dot(low, weights[part], preferred_element_type=jnp.float32)
        projected[part] = (product + biases[part : part + 1, :]).astype(jnp.bfloat16)


def project_rows(features, norms, weights, biases, block, earlier):
    rows, width = features.shape
    columns = weights.shape[2]
    whole = pl.BlockSpec(memory_space=pltpu.VMEM)
    place = pl.BlockSpec(memory_space=pl.ANY)
    return pl.pallas_call(
        project_kernel,
        grid=(1,),
        in_specs=[whole] * 4 + [place] * len(earlier),
        out_specs=[
            pl.BlockSpec((rows, width), lambda step: (block, 0)),
            pl.BlockSpec((3, rows, columns), lambda step: (0, block, 0)),
        ],
        out_shape=[
            jax.ShapeDtypeStruct((4 * rows, width), jnp.bfloat16),
            jax.ShapeDtypeStruct((3, 4 * rows, columns), jnp.bfloat16),
        ],
        input_output_aliases={4 + index: index for index in range(len(earlier))},
        compiler_params=pltpu.CompilerParams(vmem_limit_bytes=32 << 20),
        cost_estimate=pl.CostEstimate(
            flops=6 * rows * width * columns,
            bytes_accessed=4 * rows * width + 6 * (rows + width) * columns,
            transcendentals=0,
        ),
        name="project_rows",
    )(features, norms, weights, biases, *earlier)


def input_back_kernel(own, beside, across, far, grads, weights, near, low, sums, features):
    step = pl.program_id(0)
    for index, piece in enumerate((own, beside, across, far)):

        @pl.when(step == index)
        def _():
            features[...] = piece[...]

    rows = own.shape[0]
    part = pl.ds(pl.multiple_of(step * rows, rows), rows)
    product = contract_last(grads[0, part, :], weights[0])
    for index in (1, 2):
        product += contract_last(grads[index, part, :], weights[index])

    @pl.when(step % 2 == 0)
    def _():
        near[step // 2] = product

    @pl.when(step % 2 == 1)
    def _():
        low[step // 2] = product.astype(jnp.bfloat16)

    @pl.when(step == 0)
    def _():
        sums[...] = jnp.zeros_like(sums)

    scaled = normed(features[...].astype(jnp.float32))
    sums[0:1, :] += jnp.sum(product * scaled, axis=0, keepdims=True)
    sums[1:2, :] += jnp.sum(product, axis=0, keepdims=True)


def input_back(pieces, grads, weights):
    rows, width = pieces[0].shape
    columns = weights.shape[2]
    whole = pl.BlockSpec(memory_space=pltpu.VMEM)
    return pl.pallas_call(
        input_back_kernel,
        grid=(4,),
        in_specs=[whole] * 6,
        out_specs=[whole] * 3,
        out_shape=[
            jax.ShapeDtypeStruct((2, rows, width), jnp.float32),
            jax.ShapeDtypeStruct((2, rows, width), jnp.bfloat16),
            jax.ShapeDtypeStruct((8, width), jnp.float32),
        ],
        scratch_shapes=[pltpu.VMEM((rows, width), jnp.bfloat16)],
        compiler_params=pltpu.CompilerParams(vmem_limit_bytes=48 << 20),
        cost_estimate=pl.CostEstimate(
            flops=24 * rows * width * columns,
            bytes_accessed=20 * rows * width + 6 * (4 * rows + width) * columns,
            transcendentals=0,
        ),
        name="input_back",
    )(*pieces, grads, weights)


def feed_kernel(last, refs_in, *refs):
    (row_a, row_b, grad_a, grad_b, up, bias, down, *earlier) = refs[:refs_in]
    (branch_near, branch_low, mid_near, mid_low, *totals, rows_in, grads_in, up_sum, down_sum) = refs[
        refs_in:
    ]
    bias_sum = totals[-1]
    step = pl.program_id(0)
    tile = rows_in.shape[0]
    per_piece = row_a.shape[0] // tile
    part = pl.ds(pl.multiple_of((step % per_piece) * tile, tile), tile)

    @pl.when(step == 0)
    def _():
        if last:
            up_sum[...] = earlier[0][...]
            down_sum[...] = earlier[1][...]
            bias_sum[...] = earlier[2][...]
        else:
            up_sum[...] = jnp.zeros_like(up_sum)
            down_sum[...] = jnp.zeros_like(down_sum)
            bias_sum[...] = jnp.zeros_like(bias_sum)

    for index, (rows_piece, grads_piece) in enumerate(((row_a, grad_a), (row_b, grad_b))):

        @pl.when(step // per_piece == index)
        def _():
            rows_in[...] = rows_piece[part, :]
            grads_in[...] = grads_piece[part, :]

    rows, grads = rows_in[...], grads_in[...]
    hidden = jnp.dot(rows, up[...], preferred_element_type=jnp.float32) + bias[...]
    spread = 0.5 + 0.5 * lax.erf(hidden * (0.5**0.5))
    slope = spread + hidden * jnp.exp(-0.5 * hidden * hidden) * 0.3989422804014327
    active = (hidden * spread).astype(jnp.bfloat16)
    hidden_grad = contract_last(grads, down[...]) * slope
    hidden_low = hidden_grad.astype(jnp.bfloat16)
    branch = jnp.dot(active, down[...], preferred_element_type=jnp.float32)
    mid_grad = contract_last(hidden_low, up[...])
    down_sum[...] += contract_first(active, grads)
    up_sum[...] += contract_first(rows, hidden_low)
    bias_sum[0:1, :] += jnp.sum(hidden_low.astype(jnp.float32), axis=0, keepdims=True)

    @pl.when(step < per_piece)
    def _():
        branch_near[part, :] = branch
        mid_near[part, :] = mid_grad

    @pl.when(step >= per_piece)
    def _():
        branch_low[part, :] = branch.astype(jnp.bfloat16)
        mid_low[part, :] = mid_grad.astype(jnp.bfloat16)

    @pl.when(step == pl.num_programs(0) - 1)
    def _():
        if last:
            units = up_sum.shape[0]
            totals[0][:units, :] = up_sum[...].astype(jnp.bfloat16)
            totals[0][units:, :] = down_sum[...].astype(jnp.bfloat16)
        else:
            totals[0][...] = up_sum[...]
            totals[1][...] = down_sum[...]


def feed_forward(row_pair, grad_pair, up, bias, down, earlier):
    rows, width = row_pair[0].shape
    units = up.shape[1]
    last = len(earlier) > 0
    whole = pl.BlockSpec(memory_space=pltpu.VMEM)
    tile = FEED_TILE
    near = jax.ShapeDtypeStruct((rows, width), jnp.float32)
    low = jax.ShapeDtypeStruct((rows, width), jnp.bfloat16)
    if last:
        totals = [jax.ShapeDtypeStruct((width + units, width), jnp.bfloat16)]
    else:
        totals = [
            jax.ShapeDtypeStruct((width, units), jnp.float32),
            jax.ShapeDtypeStruct((units, width), jnp.float32),
        ]
    totals.append(jax.ShapeDtypeStruct((8, units), jnp.float32))
    count = 7 + len(earlier)
    return pl.pallas_call(
        functools.partial(feed_kernel, last, count),
        grid=(2 * rows // tile,),
        in_specs=[whole] * count,
        out_specs=[whole] * (4 + len(totals)),
        out_shape=[near, low, near, low] + totals,
        scratch_shapes=[
            pltpu.VMEM((tile, width), jnp.bfloat16),
            pltpu.VMEM((tile, width), jnp.bfloat16),
            pltpu.VMEM((width, units), jnp.float32),
            pltpu.VMEM((units, width), jnp.float32),
        ],
        compiler_params=pltpu.CompilerParams(vmem_limit_bytes=60 << 20),
        cost_estimate=pl.CostEstimate(
            flops=24 * rows * width * units,
            bytes_accessed=20 * rows * width + 12 * width * units,
            transcendentals=4 * rows * units,
        ),
        name="feed_forward",
    )(*row_pair, *grad_pair, up, bias, down, *earlier)


def pair_swap(array, axis, bit):
    size = lax.axis_size(axis)
    return lax.ppermute(array, axis, [(source, source ^ bit) for source in range(size)])


def gather_relative(rows):
    across = pair_swap(rows, "tensor", 2)
    beside = pair_swap(rows, "tensor", 1)
    far = pair_swap(across, "tensor", 1)
    return (rows, beside, across, far)


def finish_scatter(own, beside_low, across, far_low, gate=None):
    across = across + pair_swap(far_low, "tensor", 1).astype(jnp.float32)
    across_low = across.astype(jnp.bfloat16)
    if gate is not None:
        across_low, _ = lax.optimization_barrier((across_low, gate))
    got = pair_swap(across_low, "tensor", 2)
    own = own + pair_swap(beside_low, "tensor", 1).astype(jnp.float32)
    return own + got.astype(jnp.float32)


def scatter_relative(blocks):
    return finish_scatter(
        blocks[0], blocks[1].astype(jnp.bfloat16), blocks[2], blocks[3].astype(jnp.bfloat16)
    )


def reduce_cells(grads, bits):
    index = lax.axis_index("dp")
    block = grads
    for bit in bits:
        half = block.shape[0] // 2
        side = (index // bit) % 2
        kept = lax.dynamic_slice_in_dim(block, side * half, half, 0)
        sent = lax.dynamic_slice_in_dim(block, (1 - side) * half, half, 0)
        got = pair_swap(sent.astype(jnp.bfloat16), "dp", bit)
        block = kept + got.astype(jnp.float32)
    block = block.astype(jnp.bfloat16)
    for bit in reversed(bits):
        side = (index // bit) % 2
        got = pair_swap(block, "dp", bit)
        block = jnp.where(
            side == 0, jnp.concatenate([block, got]), jnp.concatenate([got, block])
        )
    return block.astype(jnp.float32)


def sum_cells(grads):
    bits = [1 << step for step in range((lax.axis_size("dp") - 1).bit_length())]
    half = grads.shape[0] // 2
    rotated = bits[1:] + bits[:1]
    return jnp.concatenate([reduce_cells(grads[:half], bits), reduce_cells(grads[half:], rotated)])


def sum_small(rows, axes):
    for axis in axes:
        bit = 1
        while bit < lax.axis_size(axis):
            rows = rows + pair_swap(rows, axis, bit)
            bit *= 2
    return rows


def per_device(
    cells_x,
    cotangent,
    gene_counts,
    slot_cell,
    norm_gain,
    norm_shift,
    out_bias,
    w_qkv,
    qv_bias,
    w_out,
    w_up,
    up_bias,
    w_down,
):
    rows = cells_x.shape[0]
    width = cells_x.shape[1]
    place = lax.axis_index("tensor")
    cell_ids = jnp.arange(gene_counts.shape[0], dtype=jnp.int32)
    length = jnp.sum(jnp.where(slot_cell[0] == cell_ids, gene_counts, 0))
    positions = jnp.concatenate(
        [(place ^ block) * rows + jnp.arange(rows, dtype=jnp.int32) for block in range(4)]
    )
    live_keys = positions < length
    live_rows = live_keys[:rows]
    pieces = gather_relative(cells_x)
    out_grad = jnp.where(live_rows[:, None], cotangent, jnp.zeros_like(cotangent))
    late_grad, _ = lax.optimization_barrier((out_grad, pieces[2]))
    grad_pieces = gather_relative(late_grad)
    norms_in = jnp.stack([norm_gain[0], norm_shift[0]]).astype(jnp.float32)
    biases = jnp.stack([qv_bias[0], jnp.zeros_like(qv_bias[0]), qv_bias[1]]).astype(jnp.float32)
    buffers = ()
    for block in range(4):
        buffers = project_rows(pieces[block], norms_in, w_qkv, biases, block, buffers)
    gathered_in, projected = buffers
    scalars = jnp.stack([length] + [(place ^ block) * rows for block in range(4)])
    attended_low, log_totals = attend_forward(scalars, projected)
    (attended_low, log_totals), grad_pieces = lax.optimization_barrier(
        ((attended_low, log_totals), grad_pieces)
    )

    def cut(array):
        return [array[block * rows : (block + 1) * rows] for block in range(4)]

    attn_sum = scatter_relative(
        cut(jnp.dot(attended_low, w_out, preferred_element_type=jnp.float32))
    )
    middle = cells_x.astype(jnp.float32) + attn_sum + out_bias[0].astype(jnp.float32)
    normed_mid, scaled_mid, inverse_mid = normalize(middle, norm_gain[1], norm_shift[1])
    mid_pieces = gather_relative(normed_mid.astype(jnp.bfloat16))
    up_row = up_bias.astype(jnp.float32)[None]
    branch_0, branch_1, mid_0, mid_1, *totals = feed_forward(
        mid_pieces[:2], grad_pieces[:2], w_up, up_row, w_down, ()
    )
    branch_2, branch_3, mid_2, mid_3, ffn_low, bias_sums = feed_forward(
        mid_pieces[2:], grad_pieces[2:], w_up, up_row, w_down, totals
    )
    up_bias_grad = bias_sums[0]
    ffn_grads = lax.psum(ffn_low, "dp").astype(jnp.float32)
    up_grad, down_grad = ffn_grads[:width], ffn_grads[width:]
    mid_norm_grad = finish_scatter(mid_0, mid_1, mid_2, mid_3)
    mid_back, gain_mid, shift_mid = normalize_back(
        mid_norm_grad, scaled_mid, inverse_mid, norm_gain[1]
    )
    middle_grad = out_grad.astype(jnp.float32) + mid_back
    middle_pieces = gather_relative(middle_grad.astype(jnp.bfloat16))
    middle_rows = jnp.concatenate(middle_pieces)
    branch = finish_scatter(branch_0, branch_1, branch_2, branch_3, middle_pieces[2])
    output = jnp.where(live_rows[:, None], middle + branch + out_bias[1].astype(jnp.float32), 0.0)
    block_out = output.astype(jnp.bfloat16)
    attended_grad = contract_last(middle_rows, w_out).astype(jnp.bfloat16)
    out_weight_grad = contract_first(attended_low, middle_rows)
    qkv_grad = attend_backward(scalars, projected, attended_low, attended_grad, log_totals)
    near, low, sums = input_back(pieces, qkv_grad, w_qkv)
    in_norm_grad = finish_scatter(near[0], low[0], near[1], low[1])
    qkv_weight_grad = jnp.einsum(
        "rd,src->scd", gathered_in, qkv_grad, preferred_element_type=jnp.float32
    )
    query_bias = jnp.sum(qkv_grad[0], axis=0, dtype=jnp.float32)
    value_bias = jnp.sum(qkv_grad[2], axis=0, dtype=jnp.float32)
    _, scaled_in, inverse_in = normalize(
        cells_x.astype(jnp.float32), norm_gain[0], norm_shift[0]
    )
    in_back, _, _ = normalize_back(in_norm_grad, scaled_in, inverse_in, norm_gain[0])
    input_grad = (middle_grad + in_back).astype(jnp.bfloat16)
    shared = sum_small(
        jnp.stack(
            [
                sums[0],
                gain_mid,
                sums[1],
                shift_mid,
                jnp.sum(middle_grad, axis=0),
                jnp.sum(out_grad, axis=0, dtype=jnp.float32),
            ]
        ),
        ("tensor",),
    )
    columns = w_qkv.shape[2]
    units = up_bias.shape[0]
    heavy = jnp.concatenate([out_weight_grad, qkv_weight_grad.reshape(-1, width)])
    light = jnp.concatenate([up_bias_grad, query_bias, value_bias])
    light_rows = -(-light.shape[0] // width)
    light = jnp.pad(light, (0, light_rows * width - light.shape[0])).reshape(light_rows, width)
    payload = jnp.concatenate([heavy, shared, light])
    filled = payload.shape[0]
    payload = sum_cells(jnp.pad(payload, ((0, -filled % 128), (0, 0))))
    first = heavy.shape[0]
    shared = payload[first : first + 6]
    sharded = payload[first + 6 : filled].reshape(-1)
    out_weight_grad = payload[:columns]
    qkv_weight_grad = jnp.swapaxes(payload[columns:first].reshape(3, columns, width), 1, 2)
    return (
        block_out,
        input_grad,
        shared[0:2],
        shared[2:4],
        shared[4:6],
        qkv_weight_grad,
        sharded[units : units + 2 * columns].reshape(2, columns),
        out_weight_grad,
        up_grad,
        sharded[:units],
        down_grad,
    )


def solution(mesh):
    return jax.shard_map(
        per_device,
        mesh=mesh,
        in_specs=(
            P(("dp", "tensor"), None),
            P(("dp", "tensor"), None),
            P(),
            P("dp"),
            P(),
            P(),
            P(),
            P(None, None, "tensor"),
            P(None, "tensor"),
            P("tensor", None),
            P(None, "tensor"),
            P("tensor"),
            P("tensor", None),
        ),
        out_specs=(
            P(("dp", "tensor"), None),
            P(("dp", "tensor"), None),
            P(),
            P(),
            P(),
            P(None, None, "tensor"),
            P(None, "tensor"),
            P("tensor", None),
            P(None, "tensor"),
            P("tensor"),
            P("tensor", None),
        ),
        check_vma=False,
    )
```

```python
import functools

import jax
import jax.numpy as jnp
from jax import lax
from jax.experimental import pallas as pl
from jax.experimental.pallas import tpu as pltpu
from jax.sharding import PartitionSpec as P


HEAD_DIM = 64


EPSILON = 1e-05
NEGATIVE = -1e30
FORWARD_TILE = 512
BACKWARD_TILE = 512
FEED_TILE = 256


def normalize(features, gain_row, shift_row):
    row_mean = jnp.mean(features, axis=-1, keepdims=True)
    centered = features - row_mean
    variance = jnp.mean(centered * centered, axis=-1, keepdims=True)
    inverse = lax.rsqrt(variance + EPSILON)
    scaled = centered * inverse
    return (scaled * gain_row.astype(jnp.float32) + shift_row.astype(jnp.float32), scaled, inverse)


def normalize_back(upstream, scaled, inverse, gain_row):
    graded = upstream * gain_row.astype(jnp.float32)
    grad_mean = jnp.mean(graded, axis=-1, keepdims=True)
    cross_mean = jnp.mean(graded * scaled, axis=-1, keepdims=True)
    return (
        inverse * (graded - grad_mean - scaled * cross_mean),
        jnp.sum(upstream * scaled, axis=0),
        jnp.sum(upstream, axis=0),
    )


def contract_last(left, right):
    return lax.dot_general(
        left, right, (((1,), (1,)), ((), ())), preferred_element_type=jnp.float32
    )


def contract_first(left, right):
    return lax.dot_general(
        left, right, (((0,), (0,)), ((), ())), preferred_element_type=jnp.float32
    )


def transpose_low(array):
    return jnp.transpose(array.astype(jnp.float32)).astype(jnp.bfloat16)


def fill_heads(scalars, projected, keys_aug, queries_aug):
    heads, slot_rows, _ = keys_aug.shape
    rows = slot_rows // 4
    scale = HEAD_DIM ** (-0.5)
    column = lax.broadcasted_iota(jnp.int32, (rows, HEAD_DIM), 1)
    row = lax.broadcasted_iota(jnp.int32, (rows, HEAD_DIM), 0)
    ones = jnp.where(column == 0, 1.0, 0.0).astype(jnp.bfloat16)
    for block in range(4):
        part = pl.ds(block * rows, rows)
        dead = (scalars[1 + block] + row) >= scalars[0]
        bias = jnp.where(jnp.logical_and(dead, column == 0), NEGATIVE, 0.0).astype(jnp.bfloat16)
        queries = (projected[0, part, :].astype(jnp.float32) * scale).astype(jnp.bfloat16)
        keys = projected[1, part, :]
        for head in range(heads):
            cols = slice(head * HEAD_DIM, (head + 1) * HEAD_DIM)
            queries_aug[head, part, :] = jnp.concatenate([queries[:, cols], ones], axis=1)
            keys_aug[head, part, :] = jnp.concatenate([keys[:, cols], bias], axis=1)


def attend_kernel(
    base, scalars, projected, attended, log_totals, keys_aug, queries_aug, values_t, result
):
    head, step = pl.program_id(0), pl.program_id(1)
    heads, slot_rows, _ = keys_aug.shape
    block = result.shape[1] // pl.num_programs(1)

    @pl.when(jnp.logical_and(head == 0, step == 0))
    def _():
        fill_heads(scalars, projected, keys_aug, queries_aug)
        extra = lax.broadcasted_iota(jnp.int32, (16, slot_rows), 0)
        ones = jnp.where(extra == 0, 1.0, 0.0).astype(jnp.bfloat16)
        for each in range(heads):
            cols = slice(each * HEAD_DIM, (each + 1) * HEAD_DIM)
            values_t[each, :HEAD_DIM, :] = transpose_low(projected[2, :, cols])
            values_t[each, HEAD_DIM:, :] = ones

    part = pl.ds(pl.multiple_of(step * block, block), block)
    taken = pl.ds(pl.multiple_of(base + step * block, block), block)
    scores = contract_last(keys_aug[head], queries_aug[head, taken, :])
    row_max = jnp.max(scores, axis=0, keepdims=True)
    probs = jnp.exp(scores - row_max).astype(jnp.bfloat16)
    mixed = jnp.dot(values_t[head], probs, preferred_element_type=jnp.float32)
    total = mixed[HEAD_DIM : HEAD_DIM + 1, :]
    result[head, part, :] = jnp.transpose(mixed[:HEAD_DIM, :] / total).astype(jnp.bfloat16)
    log_totals[head, :, part] = row_max + jnp.log(total)

    @pl.when(jnp.logical_and(head == heads - 1, step == pl.num_programs(1) - 1))
    def _():
        attended[...] = jnp.concatenate([result[each] for each in range(heads)], axis=1)


def attend_forward(scalars, projected, base):
    _, slot_rows, columns = projected.shape
    heads = columns // HEAD_DIM
    count = slot_rows // 2
    whole = pl.BlockSpec(memory_space=pltpu.VMEM)
    return pl.pallas_call(
        functools.partial(attend_kernel, base),
        grid_spec=pltpu.PrefetchScalarGridSpec(
            num_scalar_prefetch=1,
            grid=(heads, count // FORWARD_TILE),
            in_specs=[whole],
            out_specs=[whole, whole],
            scratch_shapes=[
                pltpu.VMEM((heads, slot_rows, 128), jnp.bfloat16),
                pltpu.VMEM((heads, slot_rows, 128), jnp.bfloat16),
                pltpu.VMEM((heads, HEAD_DIM + 16, slot_rows), jnp.bfloat16),
                pltpu.VMEM((heads, count, HEAD_DIM), jnp.bfloat16),
            ],
        ),
        out_shape=[
            jax.ShapeDtypeStruct((count, columns), jnp.bfloat16),
            jax.ShapeDtypeStruct((heads, 1, count), jnp.float32),
        ],
        compiler_params=pltpu.CompilerParams(vmem_limit_bytes=60 << 20),
        cost_estimate=pl.CostEstimate(
            flops=4 * heads * count * slot_rows * 256,
            bytes_accessed=5 * slot_rows * columns * 2,
            transcendentals=heads * count * slot_rows,
        ),
        name="attend_forward",
    )(scalars, projected)


def attend_back_kernel(last, base, scalars, projected, attended, attended_grad, log_totals, *refs):
    if last:
        earlier_queries, earlier_sums, grads, *refs = refs
        query_out, sums = None, refs[-1]
        (keys_aug, queries_aug, keys_t, values, upstream, narrow, inner, query_sum, sums) = refs
    else:
        query_out, sums, *refs = refs
        (keys_aug, queries_aug, keys_t, values, upstream, narrow, inner, query_sum) = refs
    head, step = pl.program_id(0), pl.program_id(1)
    heads, slot_rows, _ = keys_aug.shape
    count = attended.shape[0]
    block = count // pl.num_programs(1)
    every = range(heads)

    @pl.when(jnp.logical_and(head == 0, step == 0))
    def _():
        fill_heads(scalars, projected, keys_aug, queries_aug)
        if last:
            sums[...] = earlier_sums[...]
        else:
            sums[...] = jnp.zeros_like(sums)
        blank = jnp.zeros((count, HEAD_DIM), jnp.bfloat16)
        tall = jnp.zeros((slot_rows, HEAD_DIM), jnp.bfloat16)
        for each in every:
            cols = slice(each * HEAD_DIM, (each + 1) * HEAD_DIM)
            keys_t[each] = transpose_low(projected[1, :, cols])
            values[each] = jnp.concatenate([tall, projected[2, :, cols]], axis=1)
            grad = attended_grad[:, cols]
            upstream[each] = jnp.concatenate([blank, grad], axis=1)
            taken = queries_aug[each, base : base + count, :HEAD_DIM]
            narrow[each] = jnp.concatenate([taken, blank], axis=1)
            product = grad.astype(jnp.float32) * attended[:, cols].astype(jnp.float32)
            inner[each] = jnp.sum(jnp.transpose(product), axis=0, keepdims=True)

    part = pl.ds(pl.multiple_of(step * block, block), block)
    taken = pl.ds(pl.multiple_of(base + step * block, block), block)
    grad = upstream[head, part, :]
    scores = contract_last(keys_aug[head], queries_aug[head, taken, :])
    probs = jnp.exp(scores - log_totals[head, :, part])
    prob_grad = contract_last(values[head], grad)
    score_grad = (probs * (prob_grad - inner[head, :, part])).astype(jnp.bfloat16)
    sums[head] += jnp.dot(
        score_grad, narrow[head, part, :], preferred_element_type=jnp.float32
    ) + jnp.dot(probs.astype(jnp.bfloat16), grad, preferred_element_type=jnp.float32)
    query_t = jnp.dot(keys_t[head], score_grad, preferred_element_type=jnp.float32)
    scale = HEAD_DIM ** (-0.5)
    query_sum[head, part, :] = jnp.transpose(query_t * scale).astype(jnp.bfloat16)

    @pl.when(jnp.logical_and(head == heads - 1, step == pl.num_programs(1) - 1))
    def _():
        queries = jnp.concatenate([query_sum[each] for each in every], axis=1)
        if last:
            grads[0, :base, :] = earlier_queries[...]
            grads[0, base:, :] = queries
            pair = [sums[each].astype(jnp.bfloat16) for each in every]
            grads[1] = jnp.concatenate([each[:, :HEAD_DIM] for each in pair], axis=1)
            grads[2] = jnp.concatenate([each[:, HEAD_DIM:] for each in pair], axis=1)
        else:
            query_out[...] = queries


def attend_backward(scalars, projected, attended, attended_grad, log_totals, base, earlier):
    _, slot_rows, columns = projected.shape
    heads = columns // HEAD_DIM
    count = attended.shape[0]
    last = len(earlier) > 0
    whole = pl.BlockSpec(memory_space=pltpu.VMEM)
    sums = (heads, slot_rows, 2 * HEAD_DIM)
    if last:
        out_shape = jax.ShapeDtypeStruct(projected.shape, jnp.bfloat16)
        out_specs = whole
        extra = [pltpu.VMEM(sums, jnp.float32)]
    else:
        out_shape = [
            jax.ShapeDtypeStruct((count, columns), jnp.bfloat16),
            jax.ShapeDtypeStruct(sums, jnp.float32),
        ]
        out_specs = [whole, whole]
        extra = []
    return pl.pallas_call(
        functools.partial(attend_back_kernel, last, base),
        grid_spec=pltpu.PrefetchScalarGridSpec(
            num_scalar_prefetch=1,
            grid=(heads, count // BACKWARD_TILE),
            in_specs=[whole] * (4 + len(earlier)),
            out_specs=out_specs,
            scratch_shapes=[
                pltpu.VMEM((heads, slot_rows, 128), jnp.bfloat16),
                pltpu.VMEM((heads, slot_rows, 128), jnp.bfloat16),
                pltpu.VMEM((heads, HEAD_DIM, slot_rows), jnp.bfloat16),
                pltpu.VMEM((heads, slot_rows, 128), jnp.bfloat16),
                pltpu.VMEM((heads, count, 128), jnp.bfloat16),
                pltpu.VMEM((heads, count, 128), jnp.bfloat16),
                pltpu.VMEM((heads, 1, count), jnp.float32),
                pltpu.VMEM((heads, count, HEAD_DIM), jnp.bfloat16),
            ]
            + extra,
        ),
        out_shape=out_shape,
        compiler_params=pltpu.CompilerParams(vmem_limit_bytes=60 << 20),
        cost_estimate=pl.CostEstimate(
            flops=10 * heads * count * slot_rows * 256,
            bytes_accessed=8 * slot_rows * columns * 2,
            transcendentals=heads * count * slot_rows,
        ),
        name="attend_backward",
    )(scalars, projected, attended, attended_grad, log_totals, *earlier)


def normed(features):
    row_mean = jnp.mean(features, axis=-1, keepdims=True)
    centered = features - row_mean
    variance = jnp.mean(centered * centered, axis=-1, keepdims=True)
    return centered * lax.rsqrt(variance + EPSILON)


def project_kernel(features, norms, weights, biases, *refs):
    normed_rows, projected = refs[-2:]
    scaled = normed(features[...].astype(jnp.float32))
    low = (scaled * norms[0:1, :] + norms[1:2, :]).astype(jnp.bfloat16)
    normed_rows[...] = low
    for part in range(3):
        product = jnp.dot(low, weights[part], preferred_element_type=jnp.float32)
        projected[part] = (product + biases[part : part + 1, :]).astype(jnp.bfloat16)


def project_rows(features, norms, weights, biases, block, earlier):
    rows, width = features.shape
    columns = weights.shape[2]
    whole = pl.BlockSpec(memory_space=pltpu.VMEM)
    place = pl.BlockSpec(memory_space=pl.ANY)
    return pl.pallas_call(
        project_kernel,
        grid=(1,),
        in_specs=[whole] * 4 + [place] * len(earlier),
        out_specs=[
            pl.BlockSpec((rows, width), lambda step: (block, 0)),
            pl.BlockSpec((3, rows, columns), lambda step: (0, block, 0)),
        ],
        out_shape=[
            jax.ShapeDtypeStruct((4 * rows, width), jnp.bfloat16),
            jax.ShapeDtypeStruct((3, 4 * rows, columns), jnp.bfloat16),
        ],
        input_output_aliases={4 + index: index for index in range(len(earlier))},
        compiler_params=pltpu.CompilerParams(vmem_limit_bytes=32 << 20),
        cost_estimate=pl.CostEstimate(
            flops=6 * rows * width * columns,
            bytes_accessed=4 * rows * width + 6 * (rows + width) * columns,
            transcendentals=0,
        ),
        name="project_rows",
    )(features, norms, weights, biases, *earlier)


def input_back_kernel(own, beside, across, far, grads, weights, near, low, sums, features):
    step = pl.program_id(0)
    for index, piece in enumerate((own, beside, across, far)):

        @pl.when(step == index)
        def _():
            features[...] = piece[...]

    rows = own.shape[0]
    part = pl.ds(pl.multiple_of(step * rows, rows), rows)
    product = contract_last(grads[0, part, :], weights[0])
    for index in (1, 2):
        product += contract_last(grads[index, part, :], weights[index])

    @pl.when(step % 2 == 0)
    def _():
        near[step // 2] = product

    @pl.when(step % 2 == 1)
    def _():
        low[step // 2] = product.astype(jnp.bfloat16)

    @pl.when(step == 0)
    def _():
        sums[...] = jnp.zeros_like(sums)

    scaled = normed(features[...].astype(jnp.float32))
    sums[0:1, :] += jnp.sum(product * scaled, axis=0, keepdims=True)
    sums[1:2, :] += jnp.sum(product, axis=0, keepdims=True)


def input_back(pieces, grads, weights):
    rows, width = pieces[0].shape
    columns = weights.shape[2]
    whole = pl.BlockSpec(memory_space=pltpu.VMEM)
    return pl.pallas_call(
        input_back_kernel,
        grid=(4,),
        in_specs=[whole] * 6,
        out_specs=[whole] * 3,
        out_shape=[
            jax.ShapeDtypeStruct((2, rows, width), jnp.float32),
            jax.ShapeDtypeStruct((2, rows, width), jnp.bfloat16),
            jax.ShapeDtypeStruct((8, width), jnp.float32),
        ],
        scratch_shapes=[pltpu.VMEM((rows, width), jnp.bfloat16)],
        compiler_params=pltpu.CompilerParams(vmem_limit_bytes=48 << 20),
        cost_estimate=pl.CostEstimate(
            flops=24 * rows * width * columns,
            bytes_accessed=20 * rows * width + 6 * (4 * rows + width) * columns,
            transcendentals=0,
        ),
        name="input_back",
    )(*pieces, grads, weights)


def feed_kernel(last, refs_in, *refs):
    (row_a, row_b, grad_a, grad_b, up, bias, down, *earlier) = refs[:refs_in]
    (branch_near, branch_low, mid_near, mid_low, *totals, rows_in, grads_in, up_sum, down_sum) = refs[
        refs_in:
    ]
    bias_sum = totals[-1]
    step = pl.program_id(0)
    tile = rows_in.shape[0]
    per_piece = row_a.shape[0] // tile
    part = pl.ds(pl.multiple_of((step % per_piece) * tile, tile), tile)

    @pl.when(step == 0)
    def _():
        if last:
            up_sum[...] = earlier[0][...]
            down_sum[...] = earlier[1][...]
            bias_sum[...] = earlier[2][...]
        else:
            up_sum[...] = jnp.zeros_like(up_sum)
            down_sum[...] = jnp.zeros_like(down_sum)
            bias_sum[...] = jnp.zeros_like(bias_sum)

    for index, (rows_piece, grads_piece) in enumerate(((row_a, grad_a), (row_b, grad_b))):

        @pl.when(step // per_piece == index)
        def _():
            rows_in[...] = rows_piece[part, :]
            grads_in[...] = grads_piece[part, :]

    rows, grads = rows_in[...], grads_in[...]
    hidden = jnp.dot(rows, up[...], preferred_element_type=jnp.float32) + bias[...]
    spread = 0.5 + 0.5 * lax.erf(hidden * (0.5**0.5))
    slope = spread + hidden * jnp.exp(-0.5 * hidden * hidden) * 0.3989422804014327
    active = (hidden * spread).astype(jnp.bfloat16)
    hidden_grad = contract_last(grads, down[...]) * slope
    hidden_low = hidden_grad.astype(jnp.bfloat16)
    branch = jnp.dot(active, down[...], preferred_element_type=jnp.float32)
    mid_grad = contract_last(hidden_low, up[...])
    down_sum[...] += contract_first(active, grads)
    up_sum[...] += contract_first(rows, hidden_low)
    bias_sum[0:1, :] += jnp.sum(hidden_low.astype(jnp.float32), axis=0, keepdims=True)

    @pl.when(step < per_piece)
    def _():
        branch_near[part, :] = branch
        mid_near[part, :] = mid_grad

    @pl.when(step >= per_piece)
    def _():
        branch_low[part, :] = branch.astype(jnp.bfloat16)
        mid_low[part, :] = mid_grad.astype(jnp.bfloat16)

    @pl.when(step == pl.num_programs(0) - 1)
    def _():
        if last:
            units = up_sum.shape[0]
            totals[0][:units, :] = up_sum[...].astype(jnp.bfloat16)
            totals[0][units:, :] = down_sum[...].astype(jnp.bfloat16)
        else:
            totals[0][...] = up_sum[...]
            totals[1][...] = down_sum[...]


def feed_forward(row_pair, grad_pair, up, bias, down, earlier):
    rows, width = row_pair[0].shape
    units = up.shape[1]
    last = len(earlier) > 0
    whole = pl.BlockSpec(memory_space=pltpu.VMEM)
    tile = FEED_TILE
    near = jax.ShapeDtypeStruct((rows, width), jnp.float32)
    low = jax.ShapeDtypeStruct((rows, width), jnp.bfloat16)
    if last:
        totals = [jax.ShapeDtypeStruct((width + units, width), jnp.bfloat16)]
    else:
        totals = [
            jax.ShapeDtypeStruct((width, units), jnp.float32),
            jax.ShapeDtypeStruct((units, width), jnp.float32),
        ]
    totals.append(jax.ShapeDtypeStruct((8, units), jnp.float32))
    count = 7 + len(earlier)
    return pl.pallas_call(
        functools.partial(feed_kernel, last, count),
        grid=(2 * rows // tile,),
        in_specs=[whole] * count,
        out_specs=[whole] * (4 + len(totals)),
        out_shape=[near, low, near, low] + totals,
        scratch_shapes=[
            pltpu.VMEM((tile, width), jnp.bfloat16),
            pltpu.VMEM((tile, width), jnp.bfloat16),
            pltpu.VMEM((width, units), jnp.float32),
            pltpu.VMEM((units, width), jnp.float32),
        ],
        compiler_params=pltpu.CompilerParams(vmem_limit_bytes=60 << 20),
        cost_estimate=pl.CostEstimate(
            flops=24 * rows * width * units,
            bytes_accessed=20 * rows * width + 12 * width * units,
            transcendentals=4 * rows * units,
        ),
        name="feed_forward",
    )(*row_pair, *grad_pair, up, bias, down, *earlier)


def pair_swap(array, axis, bit):
    size = lax.axis_size(axis)
    return lax.ppermute(array, axis, [(source, source ^ bit) for source in range(size)])


def gather_relative(rows):
    across = pair_swap(rows, "tensor", 2)
    beside = pair_swap(rows, "tensor", 1)
    far = pair_swap(across, "tensor", 1)
    return (rows, beside, across, far)


def finish_scatter(own, beside_low, across, far_low, gate=None):
    across = across + pair_swap(far_low, "tensor", 1).astype(jnp.float32)
    across_low = across.astype(jnp.bfloat16)
    if gate is not None:
        across_low, _ = lax.optimization_barrier((across_low, gate))
    got = pair_swap(across_low, "tensor", 2)
    own = own + pair_swap(beside_low, "tensor", 1).astype(jnp.float32)
    return own + got.astype(jnp.float32)


def reduce_cells(grads, bits):
    index = lax.axis_index("dp")
    block = grads
    for bit in bits:
        half = block.shape[0] // 2
        side = (index // bit) % 2
        kept = lax.dynamic_slice_in_dim(block, side * half, half, 0)
        sent = lax.dynamic_slice_in_dim(block, (1 - side) * half, half, 0)
        got = pair_swap(sent.astype(jnp.bfloat16), "dp", bit)
        block = kept + got.astype(jnp.float32)
    block = block.astype(jnp.bfloat16)
    for bit in reversed(bits):
        side = (index // bit) % 2
        got = pair_swap(block, "dp", bit)
        block = jnp.where(
            side == 0, jnp.concatenate([block, got]), jnp.concatenate([got, block])
        )
    return block.astype(jnp.float32)


def sum_cells(grads):
    bits = [1 << step for step in range((lax.axis_size("dp") - 1).bit_length())]
    half = grads.shape[0] // 2
    rotated = bits[1:] + bits[:1]
    return jnp.concatenate([reduce_cells(grads[:half], bits), reduce_cells(grads[half:], rotated)])


def sum_small(rows, axes):
    for axis in axes:
        bit = 1
        while bit < lax.axis_size(axis):
            rows = rows + pair_swap(rows, axis, bit)
            bit *= 2
    return rows


def per_device(
    cells_x,
    cotangent,
    gene_counts,
    slot_cell,
    norm_gain,
    norm_shift,
    out_bias,
    w_qkv,
    qv_bias,
    w_out,
    w_up,
    up_bias,
    w_down,
):
    rows = cells_x.shape[0]
    width = cells_x.shape[1]
    place = lax.axis_index("tensor")
    cell_ids = jnp.arange(gene_counts.shape[0], dtype=jnp.int32)
    length = jnp.sum(jnp.where(slot_cell[0] == cell_ids, gene_counts, 0))
    positions = jnp.concatenate(
        [(place ^ block) * rows + jnp.arange(rows, dtype=jnp.int32) for block in range(4)]
    )
    live_keys = positions < length
    live_rows = live_keys[:rows]
    pieces = gather_relative(cells_x)
    out_grad = jnp.where(live_rows[:, None], cotangent, jnp.zeros_like(cotangent))
    late_grad, _ = lax.optimization_barrier((out_grad, pieces[2]))
    grad_pieces = gather_relative(late_grad)
    norms_in = jnp.stack([norm_gain[0], norm_shift[0]]).astype(jnp.float32)
    biases = jnp.stack([qv_bias[0], jnp.zeros_like(qv_bias[0]), qv_bias[1]]).astype(jnp.float32)
    buffers = ()
    for block in range(4):
        buffers = project_rows(pieces[block], norms_in, w_qkv, biases, block, buffers)
    gathered_in, projected = buffers
    scalars = jnp.stack([length] + [(place ^ block) * rows for block in range(4)])
    half = 2 * rows
    attended_far, totals_far = attend_forward(scalars, projected, half)
    attn_far = jnp.dot(attended_far, w_out, preferred_element_type=jnp.float32)
    attended_near, totals_near = attend_forward(scalars, projected, 0)
    (attended_near, totals_near), grad_pieces = lax.optimization_barrier(
        ((attended_near, totals_near), grad_pieces)
    )
    attn_near = jnp.dot(attended_near, w_out, preferred_element_type=jnp.float32)
    attn_sum = finish_scatter(
        attn_near[:rows],
        attn_near[rows:].astype(jnp.bfloat16),
        attn_far[:rows],
        attn_far[rows:].astype(jnp.bfloat16),
    )
    middle = cells_x.astype(jnp.float32) + attn_sum + out_bias[0].astype(jnp.float32)
    normed_mid, scaled_mid, inverse_mid = normalize(middle, norm_gain[1], norm_shift[1])
    mid_pieces = gather_relative(normed_mid.astype(jnp.bfloat16))
    up_row = up_bias.astype(jnp.float32)[None]
    branch_0, branch_1, mid_0, mid_1, *totals = feed_forward(
        mid_pieces[:2], grad_pieces[:2], w_up, up_row, w_down, ()
    )
    branch_2, branch_3, mid_2, mid_3, ffn_low, bias_sums = feed_forward(
        mid_pieces[2:], grad_pieces[2:], w_up, up_row, w_down, totals
    )
    up_bias_grad = bias_sums[0]
    ffn_sum = lax.psum(ffn_low, "dp")
    ffn_grads = ffn_sum.astype(jnp.float32)
    up_grad, down_grad = ffn_grads[:width], ffn_grads[width:]
    mid_norm_grad = finish_scatter(mid_0, mid_1, mid_2, mid_3)
    mid_back, gain_mid, shift_mid = normalize_back(
        mid_norm_grad, scaled_mid, inverse_mid, norm_gain[1]
    )
    middle_grad = out_grad.astype(jnp.float32) + mid_back
    middle_pieces = gather_relative(middle_grad.astype(jnp.bfloat16))
    branch = finish_scatter(branch_0, branch_1, branch_2, branch_3, middle_pieces[2])
    output = jnp.where(live_rows[:, None], middle + branch + out_bias[1].astype(jnp.float32), 0.0)
    block_out = output.astype(jnp.bfloat16)
    middle_near = jnp.concatenate(middle_pieces[:2])
    middle_far = jnp.concatenate(middle_pieces[2:])
    grad_near = contract_last(middle_near, w_out).astype(jnp.bfloat16)
    earlier = attend_backward(
        scalars, projected, attended_near, grad_near, totals_near, 0, ()
    )
    grad_far = contract_last(middle_far, w_out).astype(jnp.bfloat16)
    qkv_grad = attend_backward(
        scalars, projected, attended_far, grad_far, totals_far, half, earlier
    )
    out_weight_grad = contract_first(attended_near, middle_near) + contract_first(
        attended_far, middle_far
    )
    near, low, sums = input_back(pieces, qkv_grad, w_qkv)
    in_norm_grad = finish_scatter(near[0], low[0], near[1], low[1])
    qkv_weight_grad = jnp.einsum(
        "rd,src->scd", gathered_in, qkv_grad, preferred_element_type=jnp.float32
    )
    query_bias = jnp.sum(qkv_grad[0], axis=0, dtype=jnp.float32)
    value_bias = jnp.sum(qkv_grad[2], axis=0, dtype=jnp.float32)
    _, scaled_in, inverse_in = normalize(
        cells_x.astype(jnp.float32), norm_gain[0], norm_shift[0]
    )
    in_back, _, _ = normalize_back(in_norm_grad, scaled_in, inverse_in, norm_gain[0])
    input_grad = (middle_grad + in_back).astype(jnp.bfloat16)
    shared = sum_small(
        jnp.stack(
            [
                sums[0],
                gain_mid,
                sums[1],
                shift_mid,
                jnp.sum(middle_grad, axis=0),
                jnp.sum(out_grad, axis=0, dtype=jnp.float32),
            ]
        ),
        ("tensor",),
    )
    columns = w_qkv.shape[2]
    units = up_bias.shape[0]
    heavy = jnp.concatenate([out_weight_grad, qkv_weight_grad.reshape(-1, width)])
    light = jnp.concatenate([up_bias_grad, query_bias, value_bias])
    light_rows = -(-light.shape[0] // width)
    light = jnp.pad(light, (0, light_rows * width - light.shape[0])).reshape(light_rows, width)
    payload = jnp.concatenate([heavy, shared, light])
    filled = payload.shape[0]
    payload = sum_cells(jnp.pad(payload, ((0, -filled % 128), (0, 0))))
    first = heavy.shape[0]
    shared = payload[first : first + 6]
    sharded = payload[first + 6 : filled].reshape(-1)
    out_weight_grad = payload[:columns]
    qkv_weight_grad = jnp.swapaxes(payload[columns:first].reshape(3, columns, width), 1, 2)
    return (
        block_out,
        input_grad,
        shared[0:2],
        shared[2:4],
        shared[4:6],
        qkv_weight_grad,
        sharded[units : units + 2 * columns].reshape(2, columns),
        out_weight_grad,
        up_grad,
        sharded[:units],
        down_grad,
    )


def solution(mesh):
    return jax.shard_map(
        per_device,
        mesh=mesh,
        in_specs=(
            P(("dp", "tensor"), None),
            P(("dp", "tensor"), None),
            P(),
            P("dp"),
            P(),
            P(),
            P(),
            P(None, None, "tensor"),
            P(None, "tensor"),
            P("tensor", None),
            P(None, "tensor"),
            P("tensor"),
            P("tensor", None),
        ),
        out_specs=(
            P(("dp", "tensor"), None),
            P(("dp", "tensor"), None),
            P(),
            P(),
            P(),
            P(None, None, "tensor"),
            P(None, "tensor"),
            P("tensor", None),
            P(None, "tensor"),
            P("tensor"),
            P("tensor", None),
        ),
        check_vma=False,
    )
```
